32 devices in a mesh: groups: 2 (over y), seq: 8 (over z, x), head: 2 (over core).
Axes of the slice: x: 2, y: 2, z: 4, core: 2. Of those that a mesh axis runs over, the one named last changes fastest.
Arguments:
- queries: bfloat16 [2048, 1024], P(('groups', 'seq'), 'head'), parts along dimension 0, may hold values from -6 to 6
- key_rows: bfloat16 [2048, 2, 1024], P(('groups', 'seq'), None, 'head'), parts along dimension 0, may hold values from -6 to 6
- value_rows: bfloat16 [2048, 2, 1024], P(('groups', 'seq'), None, 'head'), parts along dimension 0, may hold values from -6 to 6
- strengths: float32 [8, 2, 2048], P('head', None, ('groups', 'seq')), parts along dimension 2, may hold values from 0.2 to 2, as said below
- log_gate: float32 [8, 2048], P('head', ('groups', 'seq')), parts along dimension 1, may hold values from -1.2 to 0, as said below
- keep_flag: int32 [2048], P(('groups', 'seq')), parts along dimension 0, may hold values 0 or 1
- norm_gain: float32 [1024], P('head'), may hold values from 0.1 to 1.9
- out_weight: bfloat16 [1024, 2048], P('head'), may hold values from -0.1875 to 0.1875
Outputs:
- projected: bfloat16 [2048, 2048], P(('groups', 'seq', 'head')), parts along dimension 0
The draws below stay inside these ranges and needn't reach their ends.
There are 2 independent parts, one for each index of `groups`. The reference program is written for one: setup_inputs(seed, part) draws one part's arguments, and reference() takes and returns one part's arrays. A program takes and returns all parts, laid end to end along the dimension named above; an argument that names none is the same for every part. Nothing has to cross between parts.
Inputs may be any that keep to these rules, and one draw needn't show every extreme that they name: `strengths`: reflection strength of each head, key and token. `log_gate`: logarithm of each head's decay at each token.
All inputs are finite; a program needn't handle non-finite values. No bound on the sum of `keep_flag` on one device may be relied on, other than what follows from the above.
Results may differ from the reference program's by a relative error of at most 0.0049.
Values may be sent and summed in bfloat16 or wider, within the bound.
A program may use at most 64 MiB of HBM per device.

```python
import math
import jax
import jax.numpy as jnp
from jax import lax

D = 2048
H = 8
DK = 128
DV = 128
BLOCK = 64
TOK_DEV = 128
SEQ = 1024


def slow_heads(key):
    ranking = jax.random.permutation(jax.random.fold_in(key, 101), H)
    return ranking < H // 2


def draw_strengths(key, part):
    slow_mask = slow_heads(key)[:, None, None]
    spread = jax.random.uniform(jax.random.fold_in(key, 7), (H, 2, SEQ), jnp.float32)
    fast_side = 0.2 + 1.6 * spread
    slow_side = 2.0 - 0.001 * spread
    return jnp.where(slow_mask, slow_side, fast_side).astype(jnp.float32)


def draw_log_gate(key, part):
    slow_mask = slow_heads(key)[:, None]
    shard_count = SEQ // TOK_DEV
    compute_speed = jnp.exp(jax.random.uniform(jax.random.fold_in(key, 11), (H, shard_count), jnp.float32, 0.0, math.log(4.0)))
    compute_speed = jnp.repeat(compute_speed, TOK_DEV, axis=1)
    items_per_second = jnp.exp(jax.random.uniform(jax.random.fold_in(key, 12), (H, SEQ), jnp.float32, math.log(0.5), 0.0))
    reference_speed = jnp.where(slow_mask, 0.15 / SEQ, 1.0 / 40.0)
    assignment_cells = jax.random.randint(jax.random.fold_in(key, 13), (2,), 0, SEQ)
    network_level_count = jax.random.uniform(jax.random.fold_in(key, 14), (2,), jnp.float32, 0.2, 0.4)
    sequence_indices = jnp.arange(SEQ)
    contiguous_span = jnp.sum(jnp.where(sequence_indices[None, :] == assignment_cells[:, None], jnp.log(1.0 - network_level_count)[:, None], 0.0), axis=0)
    return (-reference_speed * compute_speed * items_per_second + contiguous_span[None, :]).astype(jnp.float32)


def place_ends(values, rng, low, top_value):
    shape = values.shape
    index_at = [jax.random.randint(jax.random.fold_in(rng, axis), (), 0, shape[axis]) for axis in range(len(shape))]
    values = values.at[tuple(index_at)].set(low)
    longest = shape.index(max(shape))
    index_at[longest] = (index_at[longest] + 1) % shape[longest]
    return values.at[tuple(index_at)].set(top_value)


def block_levels(stream_key, extent, split, low, largest):
    def one(axis_at, parts):
        draws = jax.random.uniform(jax.random.fold_in(jax.random.fold_in(stream_key, 6), axis_at), (parts,), jnp.float32, low / len(split), largest / len(split))
        return jnp.repeat(jnp.exp(draws), extent[axis_at] // parts).reshape((-1,) + (1,) * (len(extent) - axis_at - 1))

    factor_of = one(*split[0])
    for cut in split[1:]:
        factor_of = factor_of * one(*cut)
    return factor_of


def normal_values(key, shape, deviation, limit, shards=(), kind=jnp.bfloat16):
    drawn = deviation * jax.random.normal(key, shape, jnp.float32)
    if shards:
        drawn = drawn * block_levels(key, shape, shards, -0.22, 0.18)
    return jnp.clip(drawn, -limit, limit).astype(kind)


def setup_inputs(seed: int = 0, part: int = 0) -> dict:
    key_of = jax.random.split(jax.random.key(seed), 9)
    part_keys = jax.random.split(jax.random.fold_in(key_of[8], part), 9)
    return {
        "queries": normal_values(part_keys[0], (SEQ, H * DK), 1.0, 6.0, ((0, 8), (1, 2))),
        "key_rows": normal_values(part_keys[1], (SEQ, 2, H * DK), 1.0, 6.0, ((0, 8), (2, 2))),
        "value_rows": normal_values(part_keys[2], (SEQ, 2, H * DV), 1.0, 6.0, ((0, 8), (2, 2))),
        "strengths": draw_strengths(jax.random.fold_in(jax.random.fold_in(key_of[8], part), 71), part),
        "log_gate": draw_log_gate(jax.random.fold_in(jax.random.fold_in(key_of[8], part), 71), part),
        "keep_flag": place_ends((jax.random.randint(part_keys[5], (SEQ,), 0, 4) < 3).astype(jnp.int32), jax.random.fold_in(part_keys[5], 1), 0, 1),
        "norm_gain": jnp.clip(1.0 + 0.18 * jax.random.normal(key_of[6], (H * DV,), jnp.float32), 0.1, 1.9),
        "out_weight": normal_values(key_of[7], (H * DV, D), (H * DV) ** -0.5, 0.1875, ((0, 2),)),
    }


def unit_rows(values_in):
    return values_in * lax.rsqrt(lax.optimization_barrier(jnp.sum(values_in * values_in, axis=-1, keepdims=True)) + 1e-06)

def block_pieces(q_unit, k_unit, v_rows, beta_eff, step_log):
    highest = lax.Precision.HIGHEST
    size = k_unit.shape[-2]
    query_count = q_unit.shape[-2]
    cum_log = jnp.cumsum(step_log, axis=-1)
    sequence_indices = jnp.arange(size)
    strict_lower = sequence_indices[:, None] > sequence_indices[None, :]
    lower_incl = sequence_indices[:, None] >= sequence_indices[None, :]
    log_gap = cum_log[..., :, None] - cum_log[..., None, :]
    decay_pair = jnp.where(lower_incl, jnp.exp(jnp.where(lower_incl, log_gap, 0.0)), 0.0)
    key_gram = jnp.einsum('...id,...jd->...ij', k_unit, k_unit, precision=highest)
    lower_part = jnp.where(strict_lower, beta_eff[..., :, None] * decay_pair * key_gram, 0.0)
    system = lower_part + jnp.eye(size, dtype=k_unit.dtype)
    wide_w = jax.scipy.linalg.solve_triangular(system, (beta_eff * jnp.exp(cum_log))[..., None] * k_unit, lower=True, unit_diagonal=True)
    wide_u = jax.scipy.linalg.solve_triangular(system, beta_eff[..., None] * v_rows, lower=True, unit_diagonal=True)
    last_log = cum_log[..., -1:]
    to_end = jnp.exp(last_log - cum_log)
    faded_keys = k_unit * to_end[..., None]
    eye_keys = jnp.eye(k_unit.shape[-1], dtype=k_unit.dtype)
    block_trans = jnp.exp(last_log)[..., None] * eye_keys - jnp.einsum('...ld,...le->...de', faded_keys, wide_w, precision=highest)
    block_bias = jnp.einsum('...ld,...le->...de', faded_keys, wide_u, precision=highest)
    query_log = cum_log[..., 1::2]
    query_pos = 2 * jnp.arange(query_count) + 1
    visible = query_pos[:, None] >= sequence_indices[None, :]
    query_gap = query_log[..., :, None] - cum_log[..., None, :]
    query_decay = jnp.where(visible, jnp.exp(jnp.where(visible, query_gap, 0.0)), 0.0)
    query_mix = query_decay * jnp.einsum('...td,...ld->...tl', q_unit, k_unit, precision=highest)
    local_out = jnp.einsum('...tl,...le->...te', query_mix, wide_u, precision=highest)
    reach_query = jnp.exp(query_log)[..., None] * q_unit - jnp.einsum('...tl,...ld->...td', query_mix, wide_w, precision=highest)
    return (local_out, reach_query, block_trans, block_bias)

def reference(queries, key_rows, value_rows, strengths, log_gate, keep_flag, norm_gain, out_weight):
    highest = lax.Precision.HIGHEST
    seq_len = queries.shape[0]
    head_count = strengths.shape[0]
    blocks = seq_len // BLOCK
    q_unit = unit_rows(queries.astype(jnp.float32).reshape(seq_len, head_count, DK))
    q_unit = q_unit.transpose(1, 0, 2).reshape(head_count, blocks, BLOCK, DK)
    k_unit = unit_rows(key_rows.astype(jnp.float32).reshape(seq_len, 2, head_count, DK))
    k_unit = k_unit.transpose(2, 0, 1, 3).reshape(head_count, blocks, 2 * BLOCK, DK)
    v_rows = value_rows.astype(jnp.float32).reshape(seq_len, 2, head_count, DV)
    v_rows = v_rows.transpose(2, 0, 1, 3).reshape(head_count, blocks, 2 * BLOCK, DV)
    live_flag = keep_flag.astype(jnp.float32)
    beta_eff = (strengths * live_flag[None, None, :]).transpose(0, 2, 1).reshape(head_count, blocks, 2 * BLOCK)
    first_log = log_gate * live_flag[None, :]
    step_log = jnp.stack([first_log, jnp.zeros_like(first_log)], axis=-1).reshape(head_count, blocks, 2 * BLOCK)

    def advance(state_now, pieces):
        q_block, k_block, v_block, b_block, g_block = pieces
        local_out, reach_query, block_trans, block_bias = block_pieces(q_block, k_block, v_block, b_block, g_block)
        out_rows = local_out + jnp.einsum('htd,hde->hte', reach_query, state_now, precision=highest)
        state_next = jnp.einsum('hde,hef->hdf', block_trans, state_now, precision=highest) + block_bias
        return (state_next, out_rows)
    start_state = jnp.zeros((head_count, DK, DV), jnp.float32)
    inputs_by_block = (q_unit.swapaxes(0, 1), k_unit.swapaxes(0, 1), v_rows.swapaxes(0, 1), beta_eff.swapaxes(0, 1), step_log.swapaxes(0, 1))
    _, block_outs = lax.scan(advance, start_state, inputs_by_block)
    attended = block_outs.transpose(0, 2, 1, 3).reshape(seq_len, head_count, DV)
    inv_rms = lax.rsqrt(lax.optimization_barrier(jnp.mean(attended * attended, axis=-1, keepdims=True)) + 1e-05)
    normed = (attended * inv_rms * norm_gain.reshape(head_count, DV)[None, :, :]).reshape(seq_len, head_count * DV).astype(jnp.bfloat16)
    return jnp.dot(normed.astype(jnp.float32), out_weight.astype(jnp.float32), preferred_element_type=jnp.float32).astype(jnp.bfloat16)
```

```python
import functools

import jax
import jax.numpy as jnp
from jax import lax
from jax.experimental import pallas as pl
from jax.experimental.pallas import tpu as pltpu
from jax.sharding import PartitionSpec as P

DK = 128
DV = 128
UNITS = 2
F32 = jnp.float32
BF16 = jnp.bfloat16
MESH = pl.DeviceIdType.MESH


def split2(x):
    hi = x.astype(BF16)
    return hi, (x - hi.astype(F32)).astype(BF16)


def split3(x):
    a = x.astype(BF16)
    rest = x - a.astype(F32)
    b = rest.astype(BF16)
    return a, b, (rest - b.astype(F32)).astype(BF16)


def dot(a, b):
    return jnp.dot(a, b, preferred_element_type=F32)


def dot_nt(a, b):
    return lax.dot_general(a, b, (((1,), (1,)), ((), ())), preferred_element_type=F32)


def iotas(rows, cols):
    return lax.broadcasted_iota(jnp.int32, (rows, cols), 0), lax.broadcasted_iota(jnp.int32, (rows, cols), 1)


def pair_kernel(
    heads, q_hbm, k_hbm, v_hbm, str_hbm, log_hbm, keep_hbm, gain_hbm, w_hbm, out_ref,
    k_raw, v_raw, k_ref, q_ref, str_ref, log_ref, keep_ref, gain_ref, w_own, w_oth,
    small, kt, vt, a_hi, a_lo, xt, wu, maps_hi, maps_lo, bias, got, pmap, pbias, sin, sout,
    reach_hi, reach_lo, loc, nrm, nrm_oth, acc,
    load_sem, map_send, map_recv, near_send, far_send, hop_recv, nrm_send, nrm_recv, w_send, w_recv,
):
    tok = q_ref.shape[0]
    size = 2 * tok
    n = lax.axis_size("seq")
    me = lax.axis_index("seq")
    core = lax.axis_index("head")
    sibling = 1 - core
    late = lax.rem(me, 2)
    pair = me // 2
    last_pair = n // 2 - 1
    partner = me + 1 - 2 * late
    near = lax.rem(me + 2, n)
    far = lax.rem(me + 3 - 2 * late, n)

    pairs = (
        (str_hbm, str_ref),
        (log_hbm, log_ref),
        (keep_hbm, keep_ref),
        (k_hbm, k_raw),
        (v_hbm, v_raw),
        (q_hbm, q_ref),
        (gain_hbm, gain_ref),
        (w_hbm, w_own),
    )
    loads = [pltpu.make_async_copy(a, b, load_sem.at[i]) for i, (a, b) in enumerate(pairs)]
    for load in loads:
        load.start()

    barrier = pltpu.get_barrier_semaphore()

    def signal(where):
        pl.semaphore_signal(barrier, inc=1, device_id=where, device_id_type=MESH)

    signal({"head": sibling})
    signal({"seq": partner})

    @pl.when(pair > 0)
    def _():
        signal({"seq": 2 * pair - 2})
        signal({"seq": 2 * pair - 1})

    @pl.when(pair < last_pair)
    def _():
        signal({"seq": lax.rem(2 * pair + 2, n)})
        signal({"seq": lax.rem(2 * pair + 3, n)})

    def remote(src, dst, ssem, rsem, where):
        return pltpu.make_async_remote_copy(
            src_ref=src, dst_ref=dst, send_sem=ssem, recv_sem=rsem, device_id=where, device_id_type=MESH
        )

    def give(h):
        return remote(maps_hi.at[h], got.at[h], map_send.at[h], map_recv.at[h], {"seq": partner})

    rows = DV // UNITS

    def hop(h, u, target, sems):
        span = pl.ds(u * rows, rows)
        i = h * UNITS + u
        return remote(sout.at[h, span], sin.at[h, span], sems.at[i], hop_recv.at[i], {"seq": target})

    def to_near(h, u):
        return hop(h, u, near, near_send)

    def to_far(h, u):
        return hop(h, u, far, far_send)

    half = tok // 2

    def cross(h):
        span = pl.ds(pl.multiple_of(sibling * half, half), half)
        return remote(nrm.at[h, span], nrm_oth.at[h], nrm_send.at[h], nrm_recv.at[h], {"head": sibling})

    weights = remote(w_hbm, w_oth, w_send, w_recv, {"head": sibling})

    for load in loads[:3]:
        load.wait()
    live = keep_ref[...].astype(F32)
    small[...] = jnp.zeros_like(small)
    small[:heads, :tok] = str_ref[:, 0, :] * live
    small[:heads, tok:] = str_ref[:, 1, :] * live
    small[8 : 8 + heads, :tok] = log_ref[...] * live
    r_i, c_i = iotas(size, size)
    place = jnp.where(jnp.where(r_i < tok, 2 * r_i, 2 * (r_i - tok) + 1) == c_i, 1.0, 0.0).astype(BF16)
    r_t, c_t = iotas(tok, size)
    upto = jnp.where(2 * r_t <= c_t, 1.0, 0.0).astype(BF16)
    r_c, c_c = iotas(size, tok)
    upto_c = jnp.where(2 * c_c <= r_c, 1.0, 0.0).astype(BF16)
    s3 = split3(small[...])
    beta_rows = dot(s3[0][:8], place) + (dot(s3[1][:8], place) + dot(s3[2][:8], place))
    logs = [s[8:, :tok] for s in s3]
    cum_rows = dot(logs[0], upto) + (dot(logs[1], upto) + dot(logs[2], upto))
    cum_cols = dot_nt(upto_c, logs[0]) + (dot_nt(upto_c, logs[1]) + dot_nt(upto_c, logs[2]))

    loads[3].wait()
    k_ref[...] = k_raw[...].reshape(k_ref.shape)
    row_t, col_t = iotas(tok, tok)
    after = col_t > row_t
    eye = jnp.where(row_t == col_t, 1.0, 0.0)
    betas, cums, squares = [], [], []
    for h in range(heads):
        span = slice(h * DK, (h + 1) * DK)
        kt[h] = k_ref[:, span].T
        ktf = kt[h].astype(F32)
        ss = jnp.sum(ktf * ktf, axis=0, keepdims=True) + 1e-06
        beta = beta_rows[h : h + 1]
        cum = cum_rows[h : h + 1]
        betas.append(beta)
        cums.append(cum)
        squares.append(ss)
        scale = beta / ss
        cum_col = cum_cols[:, h : h + 1]
        top = (scale * jnp.exp(jnp.minimum(cum - cum_col[:tok], 0.0))) * dot(k_ref[:tok, span], kt[h])
        low = (scale[:, tok:] * jnp.exp(jnp.minimum(cum[:, tok:] - cum_col[tok:], 0.0))) * dot(
            k_ref[tok:, span], kt[h, :, tok:]
        )
        blocks = (
            (slice(0, tok), slice(0, tok), jnp.where(after, top[:, :tok], 0.0)),
            (slice(0, tok), slice(tok, size), top[:, tok:]),
            (slice(tok, size), slice(tok, size), jnp.where(after, low, 0.0)),
        )
        for rr, cc, block in blocks:
            a_hi[h, rr, cc], a_lo[h, rr, cc] = split2(block)
            if rr == cc:
                first = jnp.where((row_t ^ col_t) == 1, block, 0.0)
                xt[h, rr, cc] = (eye - first).astype(BF16)
        zero = jnp.zeros((tok, tok), BF16)
        a_hi[h, tok:, :tok] = zero
        a_lo[h, tok:, :tok] = zero
        xt[h, tok:, :tok] = zero

    everyone = 2 + jnp.where(pair > 0, 2, 0) + jnp.where(pair < last_pair, 2, 0)
    pl.semaphore_wait(barrier, everyone)
    weights.start()

    bit = 1
    while 2 << bit <= tok:
        low_bit = row_t >> bit
        picked = jnp.where(((col_t >> bit) == (low_bit | 1)) & ((low_bit & 1) == 0), 1.0, 0.0).astype(BF16)
        for h in range(heads):
            for at in (0, tok):
                s = slice(at, at + tok)
                x = xt[h, s, s]
                y = dot(a_hi[h, s, s] * picked, x).astype(BF16)
                xt[h, s, s] = x - dot(x, y).astype(BF16)
        bit += 1
    for h in range(heads):
        y = dot(a_hi[h, :tok, tok:], xt[h, tok:, tok:]).astype(BF16)
        xt[h, :tok, tok:] = -dot(xt[h, :tok, :tok], y).astype(BF16)

    loads[4].wait()
    v_flat = v_raw[...].reshape(k_ref.shape)
    for h in range(heads):
        vt[h] = v_flat[:, h * DV : (h + 1) * DV].T

    for h in range(heads):
        beta, cum, ss = betas[h], cums[h], squares[h]
        rhs = jnp.concatenate(
            [(beta * jnp.exp(cum) / ss) * kt[h].astype(F32), (beta * lax.rsqrt(ss)) * vt[h].astype(F32)], axis=0
        )
        x = xt[h]
        w0 = dot(rhs.astype(BF16), x).astype(BF16)
        res = (rhs - w0.astype(F32)) - (dot(w0, a_hi[h]) + dot(w0, a_lo[h]))
        full = w0.astype(F32) + dot(res.astype(BF16), x)
        wu[h] = full
        last = cum[:, size - 1 : size]
        faded = split2(full * jnp.exp(last - cum))
        keys = k_ref[:, h * DK : (h + 1) * DK]
        tb = dot(faded[0], keys) + dot(faded[1], keys)
        trans = eye * jnp.exp(last) - tb[:DK]
        maps_hi[h, :DK], maps_lo[h, :DK] = split2(trans)
        maps_hi[h, DK:], maps_lo[h, DK:] = split2(tb[DK:])
        bias[h] = tb[DK:]

        @pl.when((late == 0) if h % 2 == 0 else ((late == 1) & (pair < last_pair)))
        def _():
            give(h).start()

    @pl.when(late == 0)
    def _():
        for h in range(1, heads, 2):
            give(h).start()

    loads[5].wait()
    t_i, l_i = iotas(tok, size)
    visible = l_i <= 2 * t_i + 1
    tok_r, tok_c = iotas(tok, tok)
    upto_t = jnp.where(tok_c <= tok_r, 1.0, 0.0).astype(BF16)
    cum_toks = dot_nt(upto_t, logs[0]) + (dot_nt(upto_t, logs[1]) + dot_nt(upto_t, logs[2]))
    for h in range(heads):
        q = q_ref[:, h * DK : (h + 1) * DK]
        qf = q.astype(F32)
        rq = lax.rsqrt(jnp.sum(qf * qf, axis=-1, keepdims=True) + 1e-06)
        cum_tok = cum_toks[:, h : h + 1]
        decay = jnp.where(visible, jnp.exp(jnp.minimum(cum_tok - cums[h], 0.0)), 0.0)
        mix = split2((rq * decay) * dot(q, kt[h]))
        w = split2(wu[h])
        both = dot_nt(mix[0], w[0]) + (dot_nt(mix[0], w[1]) + dot_nt(mix[1], w[0]))
        reach_hi[h], reach_lo[h] = split2((jnp.exp(cum_tok) * rq) * qf - both[:, :DK])
        loc[h] = both[:, DK:]

    def send_near(h):
        for u in range(UNITS):
            to_near(h, u).start()

    def compose(h, first, second, second_bias):
        both = dot(first[0], second[0])
        for a, b in zip(first[1:], second[1:]):
            both += dot(a, b)
        hi, lo = split2(both[:DK])
        pmap[h, :, :DK] = hi
        pmap[h, :, DK:] = lo
        pbias[h] = both[DK:] + second_bias

        @pl.when(pair == 0)
        def _():
            sout[h] = pbias[h].astype(BF16)
            send_near(h)

    @pl.when((pair < last_pair) & (late == 1))
    def _():
        for h in range(0, heads, 2):
            give(h).wait_recv()
            first = got[h]
            compose(h, (first, first), (maps_hi[h, :DK], maps_lo[h, :DK]), bias[h])

    @pl.when((pair < last_pair) & (late == 0))
    def _():
        for h in range(1, heads, 2):
            give(h).wait_recv()
            second = got[h, :DK]
            compose(h, (maps_hi[h], maps_lo[h]), (second, second), got[h, DK:].astype(F32))

    @pl.when(late == 1)
    def _():
        for h in range(heads):
            if h % 2 == 0:

                @pl.when(pair == last_pair)
                def _():
                    give(h).wait_recv()

            else:
                give(h).wait_recv()
            moved = dot_nt(reach_hi[h], got[h]) + dot_nt(reach_lo[h], got[h])
            reach_hi[h], reach_lo[h] = split2(moved[:, :DK])
            loc[h] += moved[:, DK:]

    def chain(h):
        for u in range(UNITS):
            span = slice(u * rows, (u + 1) * rows)
            to_near(h, u).wait_recv()
            moved = dot(sin[h, span], pmap[h])
            sout[h, span] = (moved[:, :DK] + moved[:, DK:] + pbias[h, span]).astype(BF16)
            to_near(h, u).start()

    for parity in range(2):

        @pl.when((pair > 0) & (pair < last_pair) & (late == 1 - parity))
        def _():
            for h in range(parity, heads, 2):
                chain(h)

        @pl.when((pair < last_pair) & (late == 1 - parity))
        def _():
            for h in range(parity, heads, 2):
                for u in range(UNITS):
                    to_far(h, u).start()

    @pl.when(pair == 0)
    def _():
        sin[...] = jnp.zeros_like(sin)

    loads[6].wait()
    loads[7].wait()

    def read(h):
        homed = (pair < last_pair) & (late == 1 - h % 2)

        @pl.when((pair > 0) & jnp.logical_not(homed))
        def _():
            for u in range(UNITS):
                to_near(h, u).wait_recv()

        state = sin[h]
        att = loc[h] + (dot_nt(reach_hi[h], state) + dot_nt(reach_lo[h], state))
        inv = lax.rsqrt(jnp.mean(att * att, axis=-1, keepdims=True) + 1e-05)
        nrm[h] = (att * inv * gain_ref[:, h * DV : (h + 1) * DV]).astype(BF16)
        cross(h).start()

    def mine(h):
        return nrm[h, pl.ds(pl.multiple_of(core * half, half), half), :]

    groups = [(h, min(h + 2, heads)) for h in range(0, heads, 2)]
    weights.wait_recv()
    for g, (lo, hi) in enumerate(groups):
        for h in range(lo, hi):
            read(h)
        span = slice(lo * DV, hi * DV)
        own = dot(jnp.concatenate([mine(h) for h in range(lo, hi)], axis=1), w_own[span, :])
        acc[...] = own if g == 0 else acc[...] + own
        for h in range(lo, hi):
            cross(h).wait_recv()
        theirs = dot(jnp.concatenate([nrm_oth[h] for h in range(lo, hi)], axis=1), w_oth[span, :])
        if g + 1 < len(groups):
            acc[...] += theirs
        else:
            out_ref[...] = (acc[...] + theirs).astype(BF16)

    for h in range(heads):
        cross(h).wait_send()
    weights.wait_send()
    for h in range(heads):

        @pl.when((late == 0) | ((pair < last_pair) if h % 2 == 1 else False))
        def _():
            give(h).wait_send()

        @pl.when((pair < last_pair) & (late == 1 - h % 2))
        def _():
            for u in range(UNITS):
                to_near(h, u).wait_send()
                to_far(h, u).wait_send()


def shards(queries, key_rows, value_rows, strengths, log_gate, keep_flag, norm_gain, out_weight):
    tok = queries.shape[0]
    heads = strengths.shape[0]
    size = 2 * tok
    wide = out_weight.shape[1]
    hbm = pl.BlockSpec(memory_space=pltpu.HBM)
    vmem = pl.BlockSpec(memory_space=pltpu.VMEM)
    dma = pltpu.SemaphoreType.DMA
    operands = (
        queries, key_rows, value_rows, strengths, log_gate, keep_flag[None, :], norm_gain[None, :], out_weight,
    )
    return pl.pallas_call(
        functools.partial(pair_kernel, heads),
        out_shape=jax.ShapeDtypeStruct((tok // 2, wide), BF16),
        in_specs=[hbm] * len(operands),
        out_specs=vmem,
        scratch_shapes=[
            pltpu.VMEM(key_rows.shape, BF16),
            pltpu.VMEM(value_rows.shape, BF16),
            pltpu.VMEM((size, heads * DK), BF16),
            pltpu.VMEM(queries.shape, BF16),
            pltpu.VMEM(strengths.shape, F32),
            pltpu.VMEM(log_gate.shape, F32),
            pltpu.VMEM((1, tok), jnp.int32),
            pltpu.VMEM((1, heads * DV), F32),
            pltpu.VMEM(out_weight.shape, BF16),
            pltpu.VMEM(out_weight.shape, BF16),
            pltpu.VMEM((16, size), F32),
            pltpu.VMEM((heads, DK, size), BF16),
            pltpu.VMEM((heads, DV, size), BF16),
            pltpu.VMEM((heads, size, size), BF16),
            pltpu.VMEM((heads, size, size), BF16),
            pltpu.VMEM((heads, size, size), BF16),
            pltpu.VMEM((heads, DK + DV, size), F32),
            pltpu.VMEM((heads, DK + DV, DK), BF16),
            pltpu.VMEM((heads, DK + DV, DK), BF16),
            pltpu.VMEM((heads, DV, DK), F32),
            pltpu.VMEM((heads, DK + DV, DK), BF16),
            pltpu.VMEM((heads, DK, 2 * DK), BF16),
            pltpu.VMEM((heads, DV, DK), F32),
            pltpu.VMEM((heads, DV, DK), BF16),
            pltpu.VMEM((heads, DV, DK), BF16),
            pltpu.VMEM((heads, tok, DK), BF16),
            pltpu.VMEM((heads, tok, DK), BF16),
            pltpu.VMEM((heads, tok, DV), F32),
            pltpu.VMEM((heads, tok, DV), BF16),
            pltpu.VMEM((heads, tok // 2, DV), BF16),
            pltpu.VMEM((tok // 2, wide), F32),
            dma((len(operands),)),
            dma((heads,)),
            dma((heads,)),
            dma((heads * UNITS,)),
            dma((heads * UNITS,)),
            dma((heads * UNITS,)),
            dma((heads,)),
            dma((heads,)),
            dma(()),
            dma(()),
        ],
        compiler_params=pltpu.CompilerParams(vmem_limit_bytes=28 << 20, collective_id=0, has_side_effects=True),
        name="pair_project",
    )(*(pltpu.with_memory_space_constraint(x, pltpu.HBM) for x in operands))


def solution(mesh):
    in_specs = (
        P(("groups", "seq"), "head"),
        P(("groups", "seq"), None, "head"),
        P(("groups", "seq"), None, "head"),
        P("head", None, ("groups", "seq")),
        P("head", ("groups", "seq")),
        P(("groups", "seq")),
        P("head"),
        P("head", None),
    )
    out_specs = P(("groups", "seq", "head"), None)
    return jax.shard_map(shards, mesh=mesh, in_specs=in_specs, out_specs=out_specs, check_vma=False)
```

```python
import functools

import jax
import jax.numpy as jnp
from jax import lax
from jax.experimental import pallas as pl
from jax.experimental.pallas import tpu as pltpu
from jax.sharding import PartitionSpec as P

DK = 128
DV = 128
UNITS = 1
F32 = jnp.float32
BF16 = jnp.bfloat16
MESH = pl.DeviceIdType.MESH


def split2(x):
    hi = x.astype(BF16)
    return hi, (x - hi.astype(F32)).astype(BF16)


def split3(x):
    a = x.astype(BF16)
    rest = x - a.astype(F32)
    b = rest.astype(BF16)
    return a, b, (rest - b.astype(F32)).astype(BF16)


def dot(a, b):
    return jnp.dot(a, b, preferred_element_type=F32)


def dot_nt(a, b):
    return lax.dot_general(a, b, (((1,), (1,)), ((), ())), preferred_element_type=F32)


def iotas(rows, cols):
    return lax.broadcasted_iota(jnp.int32, (rows, cols), 0), lax.broadcasted_iota(jnp.int32, (rows, cols), 1)


def pair_kernel(
    heads, q_hbm, k_hbm, v_hbm, str_hbm, log_hbm, keep_hbm, gain_hbm, w_hbm, out_ref,
    k_raw, v_raw, k_ref, q_ref, str_ref, log_ref, keep_ref, gain_ref, w_own, w_oth,
    small, kt, vt, a_hi, a_lo, c_top, c_low, xt, w0, res, xk, maps, bias, got, pmap, pbias, sin, sout,
    reach, loc, nrm, nrm_oth, acc,
    load_sem, map_send, map_recv, near_send, far_send, hop_recv, nrm_send, nrm_recv, w_send, w_recv,
):
    tok = q_ref.shape[0]
    size = 2 * tok
    n = lax.axis_size("seq")
    me = lax.axis_index("seq")
    core = lax.axis_index("head")
    sibling = 1 - core
    late = lax.rem(me, 2)
    pair = me // 2
    last_pair = n // 2 - 1
    partner = me + 1 - 2 * late
    near = lax.rem(me + 2, n)
    far = lax.rem(me + 3 - 2 * late, n)

    pairs = (
        (str_hbm, str_ref),
        (log_hbm, log_ref),
        (keep_hbm, keep_ref),
        (k_hbm, k_raw),
        (v_hbm, v_raw),
        (q_hbm, q_ref),
        (gain_hbm, gain_ref),
        (w_hbm, w_own),
    )
    loads = [pltpu.make_async_copy(a, b, load_sem.at[i]) for i, (a, b) in enumerate(pairs)]
    for load in loads[:7]:
        load.start()

    barrier = pltpu.get_barrier_semaphore()

    def signal(where):
        pl.semaphore_signal(barrier, inc=1, device_id=where, device_id_type=MESH)

    signal({"head": sibling})
    signal({"seq": partner})

    @pl.when(pair > 0)
    def _():
        signal({"seq": 2 * pair - 2})
        signal({"seq": 2 * pair - 1})

    @pl.when(pair < last_pair)
    def _():
        signal({"seq": lax.rem(2 * pair + 2, n)})
        signal({"seq": lax.rem(2 * pair + 3, n)})

    def remote(src, dst, ssem, rsem, where):
        return pltpu.make_async_remote_copy(
            src_ref=src, dst_ref=dst, send_sem=ssem, recv_sem=rsem, device_id=where, device_id_type=MESH
        )

    def give(h):
        return remote(maps.at[h], got.at[h], map_send.at[h], map_recv.at[h], {"seq": partner})

    def give_bias(h):
        return remote(maps.at[h, DK:], got.at[h, DK:], map_send.at[h], map_recv.at[h], {"seq": partner})

    def given(h, act):
        @pl.when(pair == 0)
        def _():
            act(give_bias(h))

        @pl.when(pair > 0)
        def _():
            act(give(h))

    rows = DV // UNITS

    def hop(h, u, target, sems):
        span = pl.ds(u * rows, rows)
        i = h * UNITS + u
        return remote(sout.at[h, span], sin.at[h, span], sems.at[i], hop_recv.at[i], {"seq": target})

    def to_near(h, u):
        return hop(h, u, near, near_send)

    def to_far(h, u):
        return hop(h, u, far, far_send)

    half = tok // 2

    def cross(h):
        span = pl.ds(pl.multiple_of(sibling * half, half), half)
        return remote(nrm.at[h, span], nrm_oth.at[h], nrm_send.at[h], nrm_recv.at[h], {"head": sibling})

    weights = remote(w_hbm, w_oth, w_send, w_recv, {"head": sibling})

    for load in loads[:3]:
        load.wait()
    live = keep_ref[...].astype(F32)
    small[...] = jnp.zeros_like(small)
    small[:heads, :tok] = str_ref[:, 0, :] * live
    small[:heads, tok:] = str_ref[:, 1, :] * live
    small[8 : 8 + heads, :tok] = log_ref[...] * live
    r_i, c_i = iotas(size, size)
    place = jnp.where(jnp.where(r_i < tok, 2 * r_i, 2 * (r_i - tok) + 1) == c_i, 1.0, 0.0).astype(BF16)
    r_t, c_t = iotas(tok, size)
    upto = jnp.where(2 * r_t <= c_t, 1.0, 0.0).astype(BF16)
    r_c, c_c = iotas(size, tok)
    upto_c = jnp.where(2 * c_c <= r_c, 1.0, 0.0).astype(BF16)
    s3 = split3(small[...])
    beta_rows = dot(s3[0][:8], place) + (dot(s3[1][:8], place) + dot(s3[2][:8], place))
    logs = [s[8:, :tok] for s in s3]
    cum_rows = dot(logs[0], upto) + (dot(logs[1], upto) + dot(logs[2], upto))
    cum_cols = dot_nt(upto_c, logs[0]) + (dot_nt(upto_c, logs[1]) + dot_nt(upto_c, logs[2]))

    loads[3].wait()
    loads[7].start()
    k_ref[...] = k_raw[...].reshape(k_ref.shape)
    row_t, col_t = iotas(tok, tok)
    after = col_t > row_t
    after_top = c_t > r_t
    eye = jnp.where(row_t == col_t, 1.0, 0.0)
    betas, cums, squares = [], [], []
    for h in range(heads):
        span = slice(h * DK, (h + 1) * DK)
        kt[h] = k_ref[:, span].T
        ktf = kt[h].astype(F32)
        ss = jnp.sum(ktf * ktf, axis=0, keepdims=True) + 1e-06
        beta = beta_rows[h : h + 1]
        cum = cum_rows[h : h + 1]
        betas.append(beta)
        cums.append(cum)
        squares.append(ss)
        scale = beta / ss
        cum_col = cum_cols[:, h : h + 1]
        top = (scale * jnp.exp(jnp.minimum(cum - cum_col[:tok], 0.0))) * dot(k_ref[:tok, span], kt[h])
        low = (scale[:, tok:] * jnp.exp(jnp.minimum(cum[:, tok:] - cum_col[tok:], 0.0))) * dot(
            k_ref[tok:, span], kt[h, :, tok:]
        )
        top = jnp.where(after_top, top, 0.0)
        low = jnp.where(after, low, 0.0)
        c_top[h] = top
        c_low[h] = low
        a_hi[h, :tok], a_lo[h, :tok] = split2(top)
        a_hi[h, tok:, tok:], a_lo[h, tok:, tok:] = split2(low)
        zero = jnp.zeros((tok, tok), BF16)
        a_hi[h, tok:, :tok] = zero
        a_lo[h, tok:, :tok] = zero
        xt[h, tok:, :tok] = zero

    everyone = 2 + jnp.where(pair > 0, 2, 0) + jnp.where(pair < last_pair, 2, 0)
    pl.semaphore_wait(barrier, everyone)
    weights.start()

    eye_b = eye.astype(BF16)
    steps = tok.bit_length() - 1
    for bit in range(steps):
        step = 1 << bit
        spans = [slice(0, tok)] if step < 16 else [slice(at, at + step) for at in range(0, tok, 2 * step)]

        def take(ref_rows):
            return jnp.concatenate([ref_rows(span) for span in spans], axis=0)

        low_bit = take(lambda span: row_t[span]) >> bit
        picked = ((take(lambda span: col_t[span]) >> bit) == (low_bit | 1)) & ((low_bit & 1) == 0)
        for h in range(heads):
            for c_ref, at in ((c_top, 0), (c_low, tok)):
                own = slice(at, at + tok)
                side = c_ref.shape[2]
                m = jnp.where(picked, take(lambda span: c_ref[h, span, :tok]), 0.0).astype(BF16)
                first = 0 if bit + 1 < steps else tok
                x = eye_b if bit == 0 else xt[h, own, own]
                parts = [c_ref[h, :, first:].astype(BF16)] if side > first else []
                parts += [x] if bit > 0 else []
                moved = dot(m, jnp.concatenate(parts, axis=1))
                if bit == 0:
                    xt[h, own, own] = x
                done = 0
                for span in spans:
                    count = span.stop - span.start
                    part = slice(done, done + count)
                    if side > first:
                        c_ref[h, span, first:] -= moved[part, : side - first]
                    gone = m[part] if bit == 0 else moved[part, side - first :].astype(BF16)
                    rows_at = slice(at + span.start, at + span.stop)
                    xt[h, rows_at, own] = x[span] - gone
                    done += count
    for h in range(heads):
        xt[h, :tok, tok:] = -dot(c_top[h, :, tok:].astype(BF16), xt[h, tok:, tok:]).astype(BF16)

    loads[4].wait()
    v_flat = v_raw[...].reshape(k_ref.shape)
    for h in range(heads):
        vt[h] = v_flat[:, h * DV : (h + 1) * DV].T

    evens, odds = range(0, heads, 2), range(1, heads, 2)

    @pl.when((pair == 0) & (late == 1))
    def _():
        got[:, :DK] = jnp.zeros((heads, DK, DK), BF16)

    for group in (odds, evens):
        rhs, fade = {}, {}
        for h in group:
            beta, cum, ss = betas[h], cums[h], squares[h]
            rhs[h] = jnp.concatenate(
                [(beta * jnp.exp(cum) / ss) * kt[h].astype(F32), (beta * lax.rsqrt(ss)) * vt[h].astype(F32)], axis=0
            )
            fade[h] = jnp.exp(cum[:, size - 1 : size] - cum)
        for h in group:
            w0[h] = dot(rhs[h].astype(BF16), xt[h]).astype(BF16)
        for h in group:
            keys = k_ref[:, h * DK : (h + 1) * DK]
            xk[h] = dot((xt[h].astype(F32) * fade[h]).astype(BF16), keys).astype(BF16)
        for h in group:
            twice = jnp.concatenate([w0[h], w0[h]], axis=1)
            res[h] = (rhs[h] - w0[h].astype(F32) - dot(twice, jnp.concatenate([a_hi[h], a_lo[h]], axis=0))).astype(BF16)
        for h in group:
            keys = k_ref[:, h * DK : (h + 1) * DK]
            faded = split2(w0[h].astype(F32) * fade[h])
            tb = dot(
                jnp.concatenate([faded[0], faded[1], res[h]], axis=1), jnp.concatenate([keys, keys, xk[h]], axis=0)
            )
            maps[h, :DK] = (eye * jnp.exp(cums[h][:, size - 1 : size]) - tb[:DK]).astype(BF16)
            maps[h, DK:] = tb[DK:].astype(BF16)
            bias[h] = tb[DK:]

        if group is odds:

            @pl.when((late == 1) & (pair < last_pair))
            def _():
                for h in odds:
                    give(h).start()

    @pl.when(late == 0)
    def _():
        for h in (*evens, *odds):
            given(h, lambda copy: copy.start())

    loads[5].wait()
    t_i, l_i = iotas(tok, size)
    visible = l_i <= 2 * t_i + 1
    tok_r, tok_c = iotas(tok, tok)
    upto_t = jnp.where(tok_c <= tok_r, 1.0, 0.0).astype(BF16)
    cum_toks = dot_nt(upto_t, logs[0]) + (dot_nt(upto_t, logs[1]) + dot_nt(upto_t, logs[2]))
    for h in range(heads):
        q = q_ref[:, h * DK : (h + 1) * DK]
        qf = q.astype(F32)
        rq = lax.rsqrt(jnp.sum(qf * qf, axis=-1, keepdims=True) + 1e-06)
        cum_tok = cum_toks[:, h : h + 1]
        decay = jnp.where(visible, jnp.exp(jnp.minimum(cum_tok - cums[h], 0.0)), 0.0)
        mix = split2((rq * decay) * dot(q, kt[h]))
        w = split2(w0[h].astype(F32) + dot(res[h], xt[h]))
        both = dot_nt(mix[0], w[0]) + (dot_nt(mix[0], w[1]) + dot_nt(mix[1], w[0]))
        reach[h, :tok], reach[h, tok:] = split2((jnp.exp(cum_tok) * rq) * qf - both[:, :DK])
        loc[h] = both[:, DK:]

    def send(h, u):
        @pl.when(pair == last_pair - 1)
        def _():
            to_far(h, u).start()

        to_near(h, u).start()

    def compose(h, first, second, second_bias):
        @pl.when(pair == 0)
        def _():
            for u in range(UNITS):
                span = slice(u * rows, (u + 1) * rows)
                sout[h, span] = (dot(first[DK + u * rows : DK + (u + 1) * rows], second) + second_bias[span]).astype(BF16)
                send(h, u)

        @pl.when(pair > 0)
        def _():
            both = dot(first, second)
            pmap[h] = both[:DK].astype(BF16)
            pbias[h] = both[DK:] + second_bias

    @pl.when((pair < last_pair) & (late == 1))
    def _():
        for h in evens:
            given(h, lambda copy: copy.wait_recv())
            compose(h, got[h], maps[h, :DK], bias[h])

    @pl.when((pair < last_pair) & (late == 0))
    def _():
        for h in odds:
            give(h).wait_recv()
            compose(h, maps[h], got[h, :DK], got[h, DK:].astype(F32))

    def chain(h):
        for u in range(UNITS):
            span = slice(u * rows, (u + 1) * rows)
            to_near(h, u).wait_recv()
            sout[h, span] = (dot(sin[h, span], pmap[h]) + pbias[h, span]).astype(BF16)
            send(h, u)

    for group, home in ((evens, 1), (odds, 0)):

        @pl.when((pair > 0) & (pair < last_pair) & (late == home))
        def _():
            for h in group:
                chain(h)

        @pl.when((pair < last_pair - 1) & (late == home))
        def _():
            for h in group:
                for u in range(UNITS):
                    to_far(h, u).start()

    @pl.when(late == 1)
    def _():
        for h in range(heads):
            if h % 2 == 0:

                @pl.when(pair == last_pair)
                def _():
                    given(h, lambda copy: copy.wait_recv())

            else:
                given(h, lambda copy: copy.wait_recv())
            moved = dot_nt(reach[h], got[h])
            moved = moved[:tok] + moved[tok:]
            reach[h, :tok], reach[h, tok:] = split2(moved[:, :DK])
            loc[h] += moved[:, DK:]

    @pl.when(pair == 0)
    def _():
        sin[...] = jnp.zeros_like(sin)

    loads[6].wait()
    loads[7].wait()

    def read(lo, hi):
        for h in range(lo, hi):
            homed = (pair < last_pair) & (late == 1 - h % 2)

            @pl.when((pair > 0) & jnp.logical_not(homed))
            def _():
                for u in range(UNITS):
                    to_near(h, u).wait_recv()

        for h in range(lo, hi):
            seen = dot_nt(reach[h], sin[h])
            att = loc[h] + (seen[:tok] + seen[tok:])
            inv = lax.rsqrt(jnp.mean(att * att, axis=-1, keepdims=True) + 1e-05)
            nrm[h] = (att * inv * gain_ref[:, h * DV : (h + 1) * DV]).astype(BF16)
        for h in range(lo, hi):
            cross(h).start()

    def mine(h):
        return nrm[h, pl.ds(pl.multiple_of(core * half, half), half), :]

    def own(lo, hi):
        return dot(jnp.concatenate([mine(h) for h in range(lo, hi)], axis=1), w_own[lo * DV : hi * DV])

    def theirs(lo, hi):
        for h in range(lo, hi):
            cross(h).wait_recv()
        return dot(jnp.concatenate([nrm_oth[h] for h in range(lo, hi)], axis=1), w_oth[lo * DV : hi * DV])

    cut = heads // 2
    read(0, cut)
    acc[...] = own(0, cut)
    read(cut, heads)
    weights.wait_recv()
    acc[...] += theirs(0, cut)
    acc[...] += own(cut, heads)
    out_ref[...] = (acc[...] + theirs(cut, heads)).astype(BF16)

    for h in range(heads):
        cross(h).wait_send()
    weights.wait_send()
    @pl.when(late == 0)
    def _():
        for h in range(heads):
            given(h, lambda copy: copy.wait_send())

    @pl.when((late == 1) & (pair < last_pair))
    def _():
        for h in odds:
            give(h).wait_send()

    for group, home in ((evens, 1), (odds, 0)):

        @pl.when((pair < last_pair) & (late == home))
        def _():
            for h in group:
                for u in range(UNITS):
                    to_near(h, u).wait_send()
                    to_far(h, u).wait_send()


def shards(queries, key_rows, value_rows, strengths, log_gate, keep_flag, norm_gain, out_weight):
    tok = queries.shape[0]
    heads = strengths.shape[0]
    size = 2 * tok
    wide = out_weight.shape[1]
    hbm = pl.BlockSpec(memory_space=pltpu.HBM)
    vmem = pl.BlockSpec(memory_space=pltpu.VMEM)
    dma = pltpu.SemaphoreType.DMA
    operands = (
        queries, key_rows, value_rows, strengths, log_gate, keep_flag[None, :], norm_gain[None, :], out_weight,
    )
    return pl.pallas_call(
        functools.partial(pair_kernel, heads),
        out_shape=jax.ShapeDtypeStruct((tok // 2, wide), BF16),
        in_specs=[hbm] * len(operands),
        out_specs=vmem,
        scratch_shapes=[
            pltpu.VMEM(key_rows.shape, BF16),
            pltpu.VMEM(value_rows.shape, BF16),
            pltpu.VMEM((size, heads * DK), BF16),
            pltpu.VMEM(queries.shape, BF16),
            pltpu.VMEM(strengths.shape, F32),
            pltpu.VMEM(log_gate.shape, F32),
            pltpu.VMEM((1, tok), jnp.int32),
            pltpu.VMEM((1, heads * DV), F32),
            pltpu.VMEM(out_weight.shape, BF16),
            pltpu.VMEM(out_weight.shape, BF16),
            pltpu.VMEM((16, size), F32),
            pltpu.VMEM((heads, DK, size), BF16),
            pltpu.VMEM((heads, DV, size), BF16),
            pltpu.VMEM((heads, size, size), BF16),
            pltpu.VMEM((heads, size, size), BF16),
            pltpu.VMEM((heads, tok, size), F32),
            pltpu.VMEM((heads, tok, tok), F32),
            pltpu.VMEM((heads, size, size), BF16),
            pltpu.VMEM((heads, DK + DV, size), BF16),
            pltpu.VMEM((heads, DK + DV, size), BF16),
            pltpu.VMEM((heads, size, DK), BF16),
            pltpu.VMEM((heads, DK + DV, DK), BF16),
            pltpu.VMEM((heads, DV, DK), F32),
            pltpu.VMEM((heads, DK + DV, DK), BF16),
            pltpu.VMEM((heads, DK, DK), BF16),
            pltpu.VMEM((heads, DV, DK), F32),
            pltpu.VMEM((heads, DV, DK), BF16),
            pltpu.VMEM((heads, DV, DK), BF16),
            pltpu.VMEM((heads, 2 * tok, DK), BF16),
            pltpu.VMEM((heads, tok, DV), F32),
            pltpu.VMEM((heads, tok, DV), BF16),
            pltpu.VMEM((heads, tok // 2, DV), BF16),
            pltpu.VMEM((tok // 2, wide), F32),
            dma((len(operands),)),
            dma((heads,)),
            dma((heads,)),
            dma((heads * UNITS,)),
            dma((heads * UNITS,)),
            dma((heads * UNITS,)),
            dma((heads,)),
            dma((heads,)),
            dma(()),
            dma(()),
        ],
        compiler_params=pltpu.CompilerParams(vmem_limit_bytes=28 << 20, collective_id=0, has_side_effects=True),
        name="pair_project",
    )(*(pltpu.with_memory_space_constraint(x, pltpu.HBM) for x in operands))


def solution(mesh):
    in_specs = (
        P(("groups", "seq"), "head"),
        P(("groups", "seq"), None, "head"),
        P(("groups", "seq"), None, "head"),
        P("head", None, ("groups", "seq")),
        P("head", ("groups", "seq")),
        P(("groups", "seq")),
        P("head"),
        P("head", None),
    )
    out_specs = P(("groups", "seq", "head"), None)
    return jax.shard_map(shards, mesh=mesh, in_specs=in_specs, out_specs=out_specs, check_vma=False)
```

```python
import functools

import jax
import jax.numpy as jnp
from jax import lax
from jax.experimental import pallas as pl
from jax.experimental.pallas import tpu as pltpu
from jax.sharding import PartitionSpec as P

DK = 128
DV = 128
F32 = jnp.float32
BF16 = jnp.bfloat16
MESH = pl.DeviceIdType.MESH


def split2(x):
    hi = x.astype(BF16)
    return hi, (x - hi.astype(F32)).astype(BF16)


def split3(x):
    a = x.astype(BF16)
    rest = x - a.astype(F32)
    b = rest.astype(BF16)
    return a, b, (rest - b.astype(F32)).astype(BF16)


def dot(a, b):
    return jnp.dot(a, b, preferred_element_type=F32)


def dot_nt(a, b):
    return lax.dot_general(a, b, (((1,), (1,)), ((), ())), preferred_element_type=F32)


def iotas(rows, cols):
    return lax.broadcasted_iota(jnp.int32, (rows, cols), 0), lax.broadcasted_iota(jnp.int32, (rows, cols), 1)


def pair_kernel(
    heads, q_hbm, k_hbm, v_hbm, str_hbm, log_hbm, keep_hbm, gain_hbm, w_hbm, out_ref,
    k_raw, v_raw, k_ref, q_ref, str_ref, log_ref, keep_ref, gain_ref, w_own, w_oth,
    small, kt, vt, a_hi, a_lo, c_top, c_low, xt, w0, res, xk, maps, bias, near_maps, far_maps, pmap, pbias, cin, sin, sout, smid,
    reach, loc, nrm, nrm_oth, acc,
    load_sem, map_send, near_recv, far_recv, mid_send, far_send, out_send, cin_recv, sin_recv,
    nrm_send, nrm_recv, w_send, w_recv,
):
    tok = q_ref.shape[0]
    size = 2 * tok
    n = lax.axis_size("seq")
    me = lax.axis_index("seq")
    core = lax.axis_index("head")
    sibling = 1 - core
    late = lax.rem(me, 2)
    pair = me // 2
    last_pair = n // 2 - 1
    partner = me + 1 - 2 * late
    near = lax.rem(me + 2, n)
    evens, odds = range(0, heads, 2), range(1, heads, 2)
    inside = pair < last_pair
    middle = inside & (pair > 0)
    homes = ((evens, inside & (late == 1) & (core == 1)), (odds, inside & (late == 0) & (core == 1)))

    pairs = (
        (str_hbm, str_ref),
        (log_hbm, log_ref),
        (keep_hbm, keep_ref),
        (k_hbm, k_raw),
        (v_hbm, v_raw),
        (q_hbm, q_ref),
        (gain_hbm, gain_ref),
        (w_hbm, w_own),
    )
    loads = [pltpu.make_async_copy(a, b, load_sem.at[i]) for i, (a, b) in enumerate(pairs)]
    for load in loads[:7]:
        load.start()

    barrier = pltpu.get_barrier_semaphore()

    def signal(where):
        pl.semaphore_signal(barrier, inc=1, device_id=where, device_id_type=MESH)

    signal({"head": sibling})
    for c in range(2):
        signal({"seq": partner, "head": c})

    @pl.when((pair < last_pair - 1) & (core == 1))
    def _():
        signal({"seq": near, "head": 1})

    @pl.when((pair == last_pair - 1) & (core == 1))
    def _():
        for c in range(2):
            signal({"seq": near, "head": c})
            signal({"seq": lax.rem(me + 3 - 2 * late, n), "head": c})

    @pl.when(middle & (core == 1))
    def _():
        signal({"seq": me - 2, "head": 1})

    @pl.when((pair == last_pair) & (pair > 0))
    def _():
        signal({"seq": me - 2, "head": 1})
        signal({"seq": me - 1 - 2 * late, "head": 1})

    peers = (
        3
        + jnp.where((pair < last_pair - 1) & (core == 1), 1, 0)
        + jnp.where((pair == last_pair - 1) & (core == 1), 4, 0)
        + jnp.where(middle & (core == 1), 1, 0)
        + jnp.where((pair == last_pair) & (pair > 0), 2, 0)
    )

    def remote(src, dst, ssem, rsem, where):
        return pltpu.make_async_remote_copy(
            src_ref=src, dst_ref=dst, send_sem=ssem, recv_sem=rsem, device_id=where, device_id_type=MESH
        )

    def flat(c, h):
        return c * heads + h

    def whole(make, act, earlier):
        if earlier:

            @pl.when(pair == 0)
            def _():
                act(make(pl.ds(DK, DV)))

            @pl.when(pair > 0)
            def _():
                act(make(pl.ds(0, DK + DV)))

        else:
            act(make(pl.ds(0, DK + DV)))

    def over(h):
        return lambda span: remote(
            maps.at[h, span], near_maps.at[h, span], map_send.at[h], near_recv.at[h], {"head": 1}
        )

    def across(c, h):
        return lambda span: remote(
            maps.at[h, span], far_maps.at[c, h, span], map_send.at[h], far_recv.at[flat(c, h)],
            {"seq": partner, "head": 1},
        )

    def to_home(h, act):
        earlier = 1 if h % 2 == 0 else 0

        @pl.when(inside & (late != earlier))
        def _():
            whole(across(core, h), act, h % 2 == 0)

        @pl.when(inside & (late == earlier) & (core == 0))
        def _():
            whole(over(h), act, h % 2 == 1)

    def to_later(h):
        return remote(
            maps.at[h], far_maps.at[core, h], map_send.at[h], far_recv.at[flat(core, h)], {"seq": partner}
        )

    def first_state(h):
        return remote(maps.at[h, pl.ds(DK, DV)], sin.at[h], mid_send.at[h], sin_recv.at[h], {"seq": partner})

    def leave(c, h, act):
        @pl.when(pair == last_pair - 1)
        def _():
            for k, target in enumerate((lax.rem(me + 3 - 2 * late, n), near)):
                act(
                    remote(
                        sout.at[c, h], sin.at[h], out_send.at[2 * flat(c, h) + k], sin_recv.at[h],
                        {"seq": target, "head": c},
                    )
                )

        @pl.when(pair < last_pair - 1)
        def _():
            act(enter(c, h))

    def enter(c, h):
        return remote(
            sout.at[c, h], cin.at[c, h], out_send.at[2 * flat(c, h)], cin_recv.at[flat(c, h)],
            {"seq": near, "head": 1},
        )

    def to_sibling(h):
        src = smid.at[0, h] if h % 2 == 0 else cin.at[0, h]
        return remote(src, sin.at[h], mid_send.at[h], sin_recv.at[h], {"head": 0})

    def to_partner(c, h):
        src = cin.at[c, h] if h % 2 == 0 else smid.at[c, h]
        return remote(src, sin.at[h], far_send.at[flat(c, h)], sin_recv.at[h], {"seq": partner, "head": c})

    half = tok // 2

    def cross(h):
        span = pl.ds(pl.multiple_of(sibling * half, half), half)
        return remote(nrm.at[h, span], nrm_oth.at[h], nrm_send.at[h], nrm_recv.at[h], {"head": sibling})

    weights = remote(w_hbm, w_oth, w_send, w_recv, {"head": sibling})

    for load in loads[:3]:
        load.wait()
    live = keep_ref[...].astype(F32)
    small[...] = jnp.zeros_like(small)
    small[:heads, :tok] = str_ref[:, 0, :] * live
    small[:heads, tok:] = str_ref[:, 1, :] * live
    small[8 : 8 + heads, :tok] = log_ref[...] * live
    r_i, c_i = iotas(size, size)
    place = jnp.where(jnp.where(r_i < tok, 2 * r_i, 2 * (r_i - tok) + 1) == c_i, 1.0, 0.0).astype(BF16)
    r_t, c_t = iotas(tok, size)
    upto = jnp.where(2 * r_t <= c_t, 1.0, 0.0).astype(BF16)
    r_c, c_c = iotas(size, tok)
    upto_c = jnp.where(2 * c_c <= r_c, 1.0, 0.0).astype(BF16)
    s3 = split3(small[...])
    beta_rows = dot(s3[0][:8], place) + (dot(s3[1][:8], place) + dot(s3[2][:8], place))
    logs = [s[8:, :tok] for s in s3]
    cum_rows = dot(logs[0], upto) + (dot(logs[1], upto) + dot(logs[2], upto))
    cum_cols = dot_nt(upto_c, logs[0]) + (dot_nt(upto_c, logs[1]) + dot_nt(upto_c, logs[2]))

    loads[3].wait()
    loads[7].start()
    k_ref[...] = k_raw[...].reshape(k_ref.shape)
    row_t, col_t = iotas(tok, tok)
    after = col_t > row_t
    after_top = c_t > r_t
    eye = jnp.where(row_t == col_t, 1.0, 0.0)
    betas, cums, squares = [], [], []
    for h in range(heads):
        span = slice(h * DK, (h + 1) * DK)
        kt[h] = k_ref[:, span].T
        ktf = kt[h].astype(F32)
        ss = jnp.sum(ktf * ktf, axis=0, keepdims=True) + 1e-06
        beta = beta_rows[h : h + 1]
        cum = cum_rows[h : h + 1]
        betas.append(beta)
        cums.append(cum)
        squares.append(ss)
        scale = beta / ss
        cum_col = cum_cols[:, h : h + 1]
        top = (scale * jnp.exp(jnp.minimum(cum - cum_col[:tok], 0.0))) * dot(k_ref[:tok, span], kt[h])
        low = (scale[:, tok:] * jnp.exp(jnp.minimum(cum[:, tok:] - cum_col[tok:], 0.0))) * dot(
            k_ref[tok:, span], kt[h, :, tok:]
        )
        top = jnp.where(after_top, top, 0.0)
        low = jnp.where(after, low, 0.0)
        c_top[h] = top
        c_low[h] = low
        a_hi[h, :tok], a_lo[h, :tok] = split2(top)
        a_hi[h, tok:, tok:], a_lo[h, tok:, tok:] = split2(low)
        zero = jnp.zeros((tok, tok), BF16)
        a_hi[h, tok:, :tok] = zero
        a_lo[h, tok:, :tok] = zero
        xt[h, tok:, :tok] = zero

    pl.semaphore_wait(barrier, peers)
    weights.start()

    eye_b = eye.astype(BF16)
    steps = tok.bit_length() - 1
    for bit in range(steps):
        step = 1 << bit
        spans = [slice(0, tok)] if step < 16 else [slice(at, at + step) for at in range(0, tok, 2 * step)]

        def take(ref_rows):
            return jnp.concatenate([ref_rows(span) for span in spans], axis=0)

        low_bit = take(lambda span: row_t[span]) >> bit
        picked = ((take(lambda span: col_t[span]) >> bit) == (low_bit | 1)) & ((low_bit & 1) == 0)
        for h in range(heads):
            for c_ref, at in ((c_top, 0), (c_low, tok)):
                own = slice(at, at + tok)
                side = c_ref.shape[2]
                m = jnp.where(picked, take(lambda span: c_ref[h, span, :tok]), 0.0).astype(BF16)
                first = 0 if bit + 1 < steps else tok
                x = eye_b if bit == 0 else xt[h, own, own]
                parts = [c_ref[h, :, first:].astype(BF16)] if side > first else []
                parts += [x] if bit > 0 else []
                moved = dot(m, jnp.concatenate(parts, axis=1))
                if bit == 0:
                    xt[h, own, own] = x
                done = 0
                for span in spans:
                    count = span.stop - span.start
                    part = slice(done, done + count)
                    if side > first:
                        c_ref[h, span, first:] -= moved[part, : side - first]
                    gone = m[part] if bit == 0 else moved[part, side - first :].astype(BF16)
                    rows_at = slice(at + span.start, at + span.stop)
                    xt[h, rows_at, own] = x[span] - gone
                    done += count
    for h in range(heads):
        xt[h, :tok, tok:] = -dot(c_top[h, :, tok:].astype(BF16), xt[h, tok:, tok:]).astype(BF16)

    loads[4].wait()
    v_flat = v_raw[...].reshape(k_ref.shape)
    for h in range(heads):
        vt[h] = v_flat[:, h * DV : (h + 1) * DV].T

    for group in (odds, evens):
        rhs, fade = {}, {}
        for h in group:
            beta, cum, ss = betas[h], cums[h], squares[h]
            rhs[h] = jnp.concatenate(
                [(beta * jnp.exp(cum) / ss) * kt[h].astype(F32), (beta * lax.rsqrt(ss)) * vt[h].astype(F32)], axis=0
            )
            fade[h] = jnp.exp(cum[:, size - 1 : size] - cum)
        for h in group:
            w0[h] = dot(rhs[h].astype(BF16), xt[h]).astype(BF16)
        for h in group:
            keys = k_ref[:, h * DK : (h + 1) * DK]
            xk[h] = dot((xt[h].astype(F32) * fade[h]).astype(BF16), keys).astype(BF16)
        for h in group:
            twice = jnp.concatenate([w0[h], w0[h]], axis=1)
            res[h] = (rhs[h] - w0[h].astype(F32) - dot(twice, jnp.concatenate([a_hi[h], a_lo[h]], axis=0))).astype(BF16)
        for h in group:
            keys = k_ref[:, h * DK : (h + 1) * DK]
            faded = split2(w0[h].astype(F32) * fade[h])
            tb = dot(
                jnp.concatenate([faded[0], faded[1], res[h]], axis=1), jnp.concatenate([keys, keys, xk[h]], axis=0)
            )
            maps[h, :DK] = (eye * jnp.exp(cums[h][:, size - 1 : size]) - tb[:DK]).astype(BF16)
            maps[h, DK:] = tb[DK:].astype(BF16)
            bias[h] = tb[DK:]

        for h in group:
            to_home(h, lambda copy: copy.start())

    @pl.when((pair == 0) & (late == 0))
    def _():
        for h in range(heads):
            first_state(h).start()

    @pl.when((pair == last_pair) & (late == 0))
    def _():
        for h in range(heads):
            to_later(h).start()

    loads[5].wait()
    t_i, l_i = iotas(tok, size)
    visible = l_i <= 2 * t_i + 1
    tok_r, tok_c = iotas(tok, tok)
    upto_t = jnp.where(tok_c <= tok_r, 1.0, 0.0).astype(BF16)
    cum_toks = dot_nt(upto_t, logs[0]) + (dot_nt(upto_t, logs[1]) + dot_nt(upto_t, logs[2]))
    for h in range(heads):
        q = q_ref[:, h * DK : (h + 1) * DK]
        qf = q.astype(F32)
        rq = lax.rsqrt(jnp.sum(qf * qf, axis=-1, keepdims=True) + 1e-06)
        cum_tok = cum_toks[:, h : h + 1]
        decay = jnp.where(visible, jnp.exp(jnp.minimum(cum_tok - cums[h], 0.0)), 0.0)
        mix = split2((rq * decay) * dot(q, kt[h]))
        w = split2(w0[h].astype(F32) + dot(res[h], xt[h]))
        both = dot_nt(mix[0], w[0]) + (dot_nt(mix[0], w[1]) + dot_nt(mix[1], w[0]))
        reach[h, :tok], reach[h, tok:] = split2((jnp.exp(cum_tok) * rq) * qf - both[:, :DK])
        loc[h] = both[:, DK:]

    for group, home in homes:

        @pl.when(home)
        def _():
            for h in group:
                for c in (1, 0):
                    if c == 0:
                        whole(over(h), lambda copy: copy.wait_recv(), h % 2 == 1)
                    whole(across(c, h), lambda copy: copy.wait_recv(), h % 2 == 0)
                    own_map = maps.at[h] if c == 1 else near_maps.at[h]
                    one, two = (far_maps.at[c, h], own_map) if h % 2 == 0 else (own_map, far_maps.at[c, h])
                    exact = c == 1 and h % 2 == 0
                    trans, shift = two[:DK], bias[h] if exact else two[DK:].astype(F32)

                    @pl.when(pair == 0)
                    def _():
                        sout[c, h] = (dot(one[DK:], trans) + shift).astype(BF16)
                        leave(c, h, lambda copy: copy.start())

                    @pl.when(pair > 0)
                    def _():
                        both = dot(one[...], trans)
                        pmap[c, h] = both[:DK].astype(BF16)
                        pbias[c, h] = both[DK:] + shift

    for group, home in homes:

        @pl.when(home & (pair > 0))
        def _():
            for h in group:
                for c in (1, 0):
                    enter(c, h).wait_recv()
                    sout[c, h] = (dot(cin[c, h], pmap[c, h]) + pbias[c, h]).astype(BF16)
                    leave(c, h, lambda copy: copy.start())
            for h in group:
                for c in (1, 0):
                    if h % 2 == 0:
                        one, shift = far_maps.at[c, h], far_maps[c, h, DK:].astype(F32)
                    elif c == 1:
                        one, shift = maps.at[h], bias[h]
                    else:
                        one, shift = near_maps.at[h], near_maps[h, DK:].astype(F32)
                    smid[c, h] = (dot(cin[c, h], one[:DK]) + shift).astype(BF16)
                    to_partner(c, h).start()
                    if c == 0:
                        to_sibling(h).start()
                    else:
                        sin[h] = smid[c, h] if h % 2 == 0 else cin[c, h]

    @pl.when((late == 1) & (pair == last_pair))
    def _():
        for h in range(heads):
            to_later(h).wait_recv()
        for h in range(heads):
            moved = dot_nt(reach[h], far_maps[core, h])
            moved = moved[:tok] + moved[tok:]
            reach[h, :tok], reach[h, tok:] = split2(moved[:, :DK])
            loc[h] += moved[:, DK:]

    @pl.when((pair == 0) & (late == 0))
    def _():
        sin[...] = jnp.zeros_like(sin)

    loads[6].wait()
    loads[7].wait()

    def read(lo, hi):
        for h in range(lo, hi):
            at_home = middle & (late == 1 - h % 2) & (core == 1)

            @pl.when(jnp.logical_not(at_home | ((pair == 0) & (late == 0))))
            def _():
                first_state(h).wait_recv()

        for h in range(lo, hi):
            seen = dot_nt(reach[h], sin[h])
            att = loc[h] + (seen[:tok] + seen[tok:])
            inv = lax.rsqrt(jnp.mean(att * att, axis=-1, keepdims=True) + 1e-05)
            nrm[h] = (att * inv * gain_ref[:, h * DV : (h + 1) * DV]).astype(BF16)
        for h in range(lo, hi):
            cross(h).start()

    def mine(h):
        return nrm[h, pl.ds(pl.multiple_of(core * half, half), half), :]

    def theirs(lo, hi):
        for h in range(lo, hi):
            cross(h).wait_recv()
        return dot(jnp.concatenate([nrm_oth[h] for h in range(lo, hi)], axis=1), w_oth[lo * DV : hi * DV])

    cut = heads // 2
    read(0, cut)
    read(cut, heads)
    acc[...] = dot(jnp.concatenate([mine(h) for h in range(heads)], axis=1), w_own[...])
    weights.wait_recv()
    acc[...] += theirs(0, cut)
    out_ref[...] = (acc[...] + theirs(cut, heads)).astype(BF16)

    for h in range(heads):
        cross(h).wait_send()
    weights.wait_send()
    for h in range(heads):
        to_home(h, lambda copy: copy.wait_send())

    @pl.when((pair == 0) & (late == 0))
    def _():
        for h in range(heads):
            first_state(h).wait_send()

    @pl.when((pair == last_pair) & (late == 0))
    def _():
        for h in range(heads):
            to_later(h).wait_send()

    for group, home in homes:

        @pl.when(home)
        def _():
            for h in group:
                for c in (1, 0):
                    leave(c, h, lambda copy: copy.wait_send())

        @pl.when(home & (pair > 0))
        def _():
            for h in group:
                to_sibling(h).wait_send()
                for c in (1, 0):
                    to_partner(c, h).wait_send()


def shards(queries, key_rows, value_rows, strengths, log_gate, keep_flag, norm_gain, out_weight):
    tok = queries.shape[0]
    heads = strengths.shape[0]
    size = 2 * tok
    wide = out_weight.shape[1]
    hbm = pl.BlockSpec(memory_space=pltpu.HBM)
    vmem = pl.BlockSpec(memory_space=pltpu.VMEM)
    dma = pltpu.SemaphoreType.DMA
    operands = (
        queries, key_rows, value_rows, strengths, log_gate, keep_flag[None, :], norm_gain[None, :], out_weight,
    )
    return pl.pallas_call(
        functools.partial(pair_kernel, heads),
        out_shape=jax.ShapeDtypeStruct((tok // 2, wide), BF16),
        in_specs=[hbm] * len(operands),
        out_specs=vmem,
        scratch_shapes=[
            pltpu.VMEM(key_rows.shape, BF16),
            pltpu.VMEM(value_rows.shape, BF16),
            pltpu.VMEM((size, heads * DK), BF16),
            pltpu.VMEM(queries.shape, BF16),
            pltpu.VMEM(strengths.shape, F32),
            pltpu.VMEM(log_gate.shape, F32),
            pltpu.VMEM((1, tok), jnp.int32),
            pltpu.VMEM((1, heads * DV), F32),
            pltpu.VMEM(out_weight.shape, BF16),
            pltpu.VMEM(out_weight.shape, BF16),
            pltpu.VMEM((16, size), F32),
            pltpu.VMEM((heads, DK, size), BF16),
            pltpu.VMEM((heads, DV, size), BF16),
            pltpu.VMEM((heads, size, size), BF16),
            pltpu.VMEM((heads, size, size), BF16),
            pltpu.VMEM((heads, tok, size), F32),
            pltpu.VMEM((heads, tok, tok), F32),
            pltpu.VMEM((heads, size, size), BF16),
            pltpu.VMEM((heads, DK + DV, size), BF16),
            pltpu.VMEM((heads, DK + DV, size), BF16),
            pltpu.VMEM((heads, size, DK), BF16),
            pltpu.VMEM((heads, DK + DV, DK), BF16),
            pltpu.VMEM((heads, DV, DK), F32),
            pltpu.VMEM((heads, DK + DV, DK), BF16),
            pltpu.VMEM((2, heads, DK + DV, DK), BF16),
            pltpu.VMEM((2, heads, DK, DK), BF16),
            pltpu.VMEM((2, heads, DV, DK), F32),
            pltpu.VMEM((2, heads, DV, DK), BF16),
            pltpu.VMEM((heads, DV, DK), BF16),
            pltpu.VMEM((2, heads, DV, DK), BF16),
            pltpu.VMEM((2, heads, DV, DK), BF16),
            pltpu.VMEM((heads, 2 * tok, DK), BF16),
            pltpu.VMEM((heads, tok, DV), F32),
            pltpu.VMEM((heads, tok, DV), BF16),
            pltpu.VMEM((heads, tok // 2, DV), BF16),
            pltpu.VMEM((tok // 2, wide), F32),
            dma((len(operands),)),
            dma((heads,)),
            dma((heads,)),
            dma((2 * heads,)),
            dma((heads,)),
            dma((2 * heads,)),
            dma((4 * heads,)),
            dma((2 * heads,)),
            dma((heads,)),
            dma((heads,)),
            dma((heads,)),
            dma(()),
            dma(()),
        ],
        compiler_params=pltpu.CompilerParams(vmem_limit_bytes=28 << 20, collective_id=0, has_side_effects=True),
        name="pair_project",
    )(*(pltpu.with_memory_space_constraint(x, pltpu.HBM) for x in operands))


def solution(mesh):
    in_specs = (
        P(("groups", "seq"), "head"),
        P(("groups", "seq"), None, "head"),
        P(("groups", "seq"), None, "head"),
        P("head", None, ("groups", "seq")),
        P("head", ("groups", "seq")),
        P(("groups", "seq")),
        P("head"),
        P("head", None),
    )
    out_specs = P(("groups", "seq", "head"), None)
    return jax.shard_map(shards, mesh=mesh, in_specs=in_specs, out_specs=out_specs, check_vma=False)
```

```python
import functools

import jax
import jax.numpy as jnp
from jax import lax
from jax.experimental import pallas as pl
from jax.experimental.pallas import tpu as pltpu
from jax.sharding import PartitionSpec as P

DK = 128
DV = 128
F32 = jnp.float32
BF16 = jnp.bfloat16
MESH = pl.DeviceIdType.MESH


def split2(x):
    hi = x.astype(BF16)
    return hi, (x - hi.astype(F32)).astype(BF16)


def split3(x):
    a = x.astype(BF16)
    rest = x - a.astype(F32)
    b = rest.astype(BF16)
    return a, b, (rest - b.astype(F32)).astype(BF16)


def dot(a, b):
    return jnp.dot(a, b, preferred_element_type=F32)


def dot_nt(a, b):
    return lax.dot_general(a, b, (((1,), (1,)), ((), ())), preferred_element_type=F32)


def iotas(rows, cols):
    return lax.broadcasted_iota(jnp.int32, (rows, cols), 0), lax.broadcasted_iota(jnp.int32, (rows, cols), 1)


def pair_kernel(
    heads, q_hbm, k_hbm, v_hbm, str_hbm, log_hbm, keep_hbm, gain_hbm, w_hbm, out_ref,
    k_raw, v_raw, k_ref, q_ref, str_ref, log_ref, keep_ref, gain_ref, w_own, w_oth,
    small, kt, vt, a_hi, a_lo, c_top, c_low, xt, w0, res, xk, maps, bias, near_maps, far_maps, pmap, pbias, cin, sin, sout, smid,
    reach, loc, nrm, nrm_oth, acc,
    load_sem, map_send, near_recv, far_recv, mid_send, far_send, out_send, cin_recv, sin_recv,
    nrm_send, nrm_recv, w_send, w_recv,
):
    tok = q_ref.shape[0]
    size = 2 * tok
    n = lax.axis_size("seq")
    me = lax.axis_index("seq")
    core = lax.axis_index("head")
    sibling = 1 - core
    late = lax.rem(me, 2)
    pair = me // 2
    last_pair = n // 2 - 1
    partner = me + 1 - 2 * late
    near = lax.rem(me + 2, n)
    evens, odds = range(0, heads, 2), range(1, heads, 2)
    inside = pair < last_pair
    middle = inside & (pair > 0)
    homes = ((evens, inside & (late == 1) & (core == 1)), (odds, inside & (late == 0) & (core == 1)))

    pairs = (
        (str_hbm, str_ref),
        (log_hbm, log_ref),
        (keep_hbm, keep_ref),
        (k_hbm, k_raw),
        (v_hbm, v_raw),
        (q_hbm, q_ref),
        (gain_hbm, gain_ref),
        (w_hbm, w_own),
    )
    loads = [pltpu.make_async_copy(a, b, load_sem.at[i]) for i, (a, b) in enumerate(pairs)]
    for load in loads[:7]:
        load.start()

    barrier = pltpu.get_barrier_semaphore()

    def signal(where):
        pl.semaphore_signal(barrier, inc=1, device_id=where, device_id_type=MESH)

    signal({"head": sibling})
    for c in range(2):
        signal({"seq": partner, "head": c})

    @pl.when((pair < last_pair - 1) & (core == 1))
    def _():
        signal({"seq": near, "head": 1})

    @pl.when((pair == last_pair - 1) & (core == 1))
    def _():
        for c in range(2):
            signal({"seq": near, "head": c})
            signal({"seq": lax.rem(me + 3 - 2 * late, n), "head": c})

    @pl.when(middle & (core == 1))
    def _():
        signal({"seq": me - 2, "head": 1})

    @pl.when((pair == last_pair) & (pair > 0))
    def _():
        signal({"seq": me - 2, "head": 1})
        signal({"seq": me - 1 - 2 * late, "head": 1})

    peers = (
        3
        + jnp.where((pair < last_pair - 1) & (core == 1), 1, 0)
        + jnp.where((pair == last_pair - 1) & (core == 1), 4, 0)
        + jnp.where(middle & (core == 1), 1, 0)
        + jnp.where((pair == last_pair) & (pair > 0), 2, 0)
    )

    def remote(src, dst, ssem, rsem, where):
        return pltpu.make_async_remote_copy(
            src_ref=src, dst_ref=dst, send_sem=ssem, recv_sem=rsem, device_id=where, device_id_type=MESH
        )

    def flat(c, h):
        return c * heads + h

    def whole(make, act, earlier):
        if earlier:

            @pl.when(pair == 0)
            def _():
                act(make(pl.ds(DK, DV)))

            @pl.when(pair > 0)
            def _():
                act(make(pl.ds(0, DK + DV)))

        else:
            act(make(pl.ds(0, DK + DV)))

    def over(h):
        return lambda span: remote(
            maps.at[h, span], near_maps.at[h, span], map_send.at[h], near_recv.at[h], {"head": 1}
        )

    def across(c, h):
        return lambda span: remote(
            maps.at[h, span], far_maps.at[c, h, span], map_send.at[h], far_recv.at[flat(c, h)],
            {"seq": partner, "head": 1},
        )

    def to_home(h, act):
        earlier = 1 if h % 2 == 0 else 0

        @pl.when(inside & (late != earlier))
        def _():
            whole(across(core, h), act, h % 2 == 0)

        @pl.when(inside & (late == earlier) & (core == 0))
        def _():
            whole(over(h), act, h % 2 == 1)

    def to_later(h):
        return remote(
            maps.at[h], far_maps.at[core, h], map_send.at[h], far_recv.at[flat(core, h)], {"seq": partner}
        )

    def first_state(h):
        return remote(maps.at[h, pl.ds(DK, DV)], sin.at[h], mid_send.at[h], sin_recv.at[h], {"seq": partner})

    def leave(c, h, act):
        @pl.when(pair == last_pair - 1)
        def _():
            for k, target in enumerate((lax.rem(me + 3 - 2 * late, n), near)):
                act(
                    remote(
                        sout.at[c, h], sin.at[h], out_send.at[2 * flat(c, h) + k], sin_recv.at[h],
                        {"seq": target, "head": c},
                    )
                )

        @pl.when(pair < last_pair - 1)
        def _():
            act(enter(c, h))

    def enter(c, h):
        return remote(
            sout.at[c, h], cin.at[c, h], out_send.at[2 * flat(c, h)], cin_recv.at[flat(c, h)],
            {"seq": near, "head": 1},
        )

    def to_sibling(h):
        src = smid.at[0, h] if h % 2 == 0 else cin.at[0, h]
        return remote(src, sin.at[h], mid_send.at[h], sin_recv.at[h], {"head": 0})

    def to_partner(c, h):
        src = cin.at[c, h] if h % 2 == 0 else smid.at[c, h]
        return remote(src, sin.at[h], far_send.at[flat(c, h)], sin_recv.at[h], {"seq": partner, "head": c})

    half = tok // 2

    def cross(h):
        span = pl.ds(pl.multiple_of(sibling * half, half), half)
        return remote(nrm.at[h, span], nrm_oth.at[h], nrm_send.at[h], nrm_recv.at[h], {"head": sibling})

    weights = remote(w_hbm, w_oth, w_send, w_recv, {"head": sibling})

    for load in loads[:3]:
        load.wait()
    live = keep_ref[...].astype(F32)
    small[...] = jnp.zeros_like(small)
    small[:heads, :tok] = str_ref[:, 0, :] * live
    small[:heads, tok:] = str_ref[:, 1, :] * live
    small[8 : 8 + heads, :tok] = log_ref[...] * live
    r_i, c_i = iotas(size, size)
    place = jnp.where(jnp.where(r_i < tok, 2 * r_i, 2 * (r_i - tok) + 1) == c_i, 1.0, 0.0).astype(BF16)
    r_t, c_t = iotas(tok, size)
    upto = jnp.where(2 * r_t <= c_t, 1.0, 0.0).astype(BF16)
    r_c, c_c = iotas(size, tok)
    upto_c = jnp.where(2 * c_c <= r_c, 1.0, 0.0).astype(BF16)
    s3 = split3(small[...])
    beta_rows = dot(s3[0][:8], place) + (dot(s3[1][:8], place) + dot(s3[2][:8], place))
    logs = [s[8:, :tok] for s in s3]
    cum_rows = dot(logs[0], upto) + (dot(logs[1], upto) + dot(logs[2], upto))
    cum_cols = dot_nt(upto_c, logs[0]) + (dot_nt(upto_c, logs[1]) + dot_nt(upto_c, logs[2]))

    loads[3].wait()
    loads[7].start()
    k_ref[...] = k_raw[...].reshape(k_ref.shape)
    row_t, col_t = iotas(tok, tok)
    after = col_t > row_t
    after_top = c_t > r_t
    eye = jnp.where(row_t == col_t, 1.0, 0.0)
    betas, cums, squares = [], [], []
    for h in range(heads):
        span = slice(h * DK, (h + 1) * DK)
        kt[h] = k_ref[:, span].T
        ktf = kt[h].astype(F32)
        ss = jnp.sum(ktf * ktf, axis=0, keepdims=True) + 1e-06
        beta = beta_rows[h : h + 1]
        cum = cum_rows[h : h + 1]
        betas.append(beta)
        cums.append(cum)
        squares.append(ss)
        scale = beta / ss
        cum_col = cum_cols[:, h : h + 1]
        top = (scale * jnp.exp(jnp.minimum(cum - cum_col[:tok], 0.0))) * dot(k_ref[:tok, span], kt[h])
        low = (scale[:, tok:] * jnp.exp(jnp.minimum(cum[:, tok:] - cum_col[tok:], 0.0))) * dot(
            k_ref[tok:, span], kt[h, :, tok:]
        )
        top = jnp.where(after_top, top, 0.0)
        low = jnp.where(after, low, 0.0)
        c_top[h] = top
        c_low[h] = low
        a_hi[h, :tok], a_lo[h, :tok] = split2(top)
        a_hi[h, tok:, tok:], a_lo[h, tok:, tok:] = split2(low)
        zero = jnp.zeros((tok, tok), BF16)
        a_hi[h, tok:, :tok] = zero
        a_lo[h, tok:, :tok] = zero
        xt[h, tok:, :tok] = zero

    pl.semaphore_wait(barrier, peers)
    weights.start()

    eye_b = eye.astype(BF16)
    steps = tok.bit_length() - 1
    for bit in range(steps):
        step = 1 << bit
        spans = [slice(0, tok)] if step < 16 else [slice(at, at + step) for at in range(0, tok, 2 * step)]

        def take(ref_rows):
            return jnp.concatenate([ref_rows(span) for span in spans], axis=0)

        low_bit = take(lambda span: row_t[span]) >> bit
        picked = ((take(lambda span: col_t[span]) >> bit) == (low_bit | 1)) & ((low_bit & 1) == 0)
        for h in range(heads):
            for c_ref, at in ((c_top, 0), (c_low, tok)):
                own = slice(at, at + tok)
                side = c_ref.shape[2]
                m = jnp.where(picked, take(lambda span: c_ref[h, span, :tok]), 0.0).astype(BF16)
                first = 0 if bit + 1 < steps else tok
                x = eye_b if bit == 0 else xt[h, own, own]
                if step < 16:
                    c_hi, c_lo = split2(c_ref[h])
                    if bit > 0:
                        c_hi = jnp.concatenate([c_hi, x], axis=1)
                        c_lo = jnp.concatenate([c_lo, jnp.zeros_like(x)], axis=1)
                    moved = dot(jnp.concatenate([m, m], axis=1), jnp.concatenate([c_hi, c_lo], axis=0))
                elif side > first:
                    moved = dot(m, jnp.concatenate([c_ref[h, :, first:].astype(BF16), x], axis=1))
                else:
                    moved = dot(m, x)
                if bit == 0:
                    xt[h, own, own] = x
                done = 0
                for span in spans:
                    count = span.stop - span.start
                    part = slice(done, done + count)
                    if side > first:
                        c_ref[h, span, first:] -= moved[part, : side - first]
                    gone = m[part] if bit == 0 else moved[part, side - first :].astype(BF16)
                    rows_at = slice(at + span.start, at + span.stop)
                    xt[h, rows_at, own] = x[span] - gone
                    done += count
    for h in range(heads):
        xt[h, :tok, tok:] = -dot(c_top[h, :, tok:].astype(BF16), xt[h, tok:, tok:]).astype(BF16)

    loads[4].wait()
    v_flat = v_raw[...].reshape(k_ref.shape)
    for h in range(heads):
        vt[h] = v_flat[:, h * DV : (h + 1) * DV].T

    for group in (odds, evens):
        rhs, fade = {}, {}
        for h in group:
            beta, cum, ss = betas[h], cums[h], squares[h]
            rhs[h] = jnp.concatenate(
                [(beta * jnp.exp(cum) / ss) * kt[h].astype(F32), (beta * lax.rsqrt(ss)) * vt[h].astype(F32)], axis=0
            )
            fade[h] = jnp.exp(cum[:, size - 1 : size] - cum)
        for h in group:
            w0[h] = dot(rhs[h].astype(BF16), xt[h]).astype(BF16)
        for h in group:
            keys = k_ref[:, h * DK : (h + 1) * DK]
            xk[h] = dot((xt[h].astype(F32) * fade[h]).astype(BF16), keys).astype(BF16)
        for h in group:
            twice = jnp.concatenate([w0[h], w0[h]], axis=1)
            res[h] = (rhs[h] - w0[h].astype(F32) - dot(twice, jnp.concatenate([a_hi[h], a_lo[h]], axis=0))).astype(BF16)
        for h in group:
            keys = k_ref[:, h * DK : (h + 1) * DK]
            faded = split2(w0[h].astype(F32) * fade[h])
            tb = dot(
                jnp.concatenate([faded[0], faded[1], res[h]], axis=1), jnp.concatenate([keys, keys, xk[h]], axis=0)
            )
            maps[h, :DK] = (eye * jnp.exp(cums[h][:, size - 1 : size]) - tb[:DK]).astype(BF16)
            maps[h, DK:] = tb[DK:].astype(BF16)
            bias[h] = tb[DK:]

        for h in group:
            to_home(h, lambda copy: copy.start())

    @pl.when((pair == 0) & (late == 0))
    def _():
        for h in range(heads):
            first_state(h).start()

    @pl.when((pair == last_pair) & (late == 0))
    def _():
        for h in range(heads):
            to_later(h).start()

    loads[5].wait()
    t_i, l_i = iotas(tok, size)
    visible = l_i <= 2 * t_i + 1
    tok_r, tok_c = iotas(tok, tok)
    upto_t = jnp.where(tok_c <= tok_r, 1.0, 0.0).astype(BF16)
    cum_toks = dot_nt(upto_t, logs[0]) + (dot_nt(upto_t, logs[1]) + dot_nt(upto_t, logs[2]))
    for h in range(heads):
        q = q_ref[:, h * DK : (h + 1) * DK]
        qf = q.astype(F32)
        rq = lax.rsqrt(jnp.sum(qf * qf, axis=-1, keepdims=True) + 1e-06)
        cum_tok = cum_toks[:, h : h + 1]
        decay = jnp.where(visible, jnp.exp(jnp.minimum(cum_tok - cums[h], 0.0)), 0.0)
        mix = split2((rq * decay) * dot(q, kt[h]))
        w = split2(w0[h].astype(F32) + dot(res[h], xt[h]))
        both = dot_nt(mix[0], w[0]) + (dot_nt(mix[0], w[1]) + dot_nt(mix[1], w[0]))
        reach[h, :tok], reach[h, tok:] = split2((jnp.exp(cum_tok) * rq) * qf - both[:, :DK])
        loc[h] = both[:, DK:]

    for group, home in homes:

        @pl.when(home)
        def _():
            for h in group:
                for c in (1, 0):
                    if c == 0:
                        whole(over(h), lambda copy: copy.wait_recv(), h % 2 == 1)
                    whole(across(c, h), lambda copy: copy.wait_recv(), h % 2 == 0)
                    own_map = maps.at[h] if c == 1 else near_maps.at[h]
                    one, two = (far_maps.at[c, h], own_map) if h % 2 == 0 else (own_map, far_maps.at[c, h])
                    exact = c == 1 and h % 2 == 0
                    trans, shift = two[:DK], bias[h] if exact else two[DK:].astype(F32)

                    @pl.when(pair == 0)
                    def _():
                        sout[c, h] = (dot(one[DK:], trans) + shift).astype(BF16)
                        leave(c, h, lambda copy: copy.start())

                    @pl.when(pair > 0)
                    def _():
                        both = dot(one[...], trans)
                        pmap[c, h] = both[:DK].astype(BF16)
                        pbias[c, h] = both[DK:] + shift

    for group, home in homes:

        @pl.when(home & (pair > 0))
        def _():
            for h in group:
                for c in (1, 0):
                    enter(c, h).wait_recv()
                    sout[c, h] = (dot(cin[c, h], pmap[c, h]) + pbias[c, h]).astype(BF16)
                    leave(c, h, lambda copy: copy.start())
                    if h % 2 == 0:
                        to_partner(c, h).start()
                    elif c == 0:
                        to_sibling(h).start()
                    else:
                        sin[h] = cin[c, h]
                for c in (1, 0):
                    if h % 2 == 0:
                        one, shift = far_maps.at[c, h], far_maps[c, h, DK:].astype(F32)
                    elif c == 1:
                        one, shift = maps.at[h], bias[h]
                    else:
                        one, shift = near_maps.at[h], near_maps[h, DK:].astype(F32)
                    smid[c, h] = (dot(cin[c, h], one[:DK]) + shift).astype(BF16)
                    if h % 2 == 1:
                        to_partner(c, h).start()
                    elif c == 0:
                        to_sibling(h).start()
                    else:
                        sin[h] = smid[c, h]

    @pl.when((late == 1) & (pair == last_pair))
    def _():
        for h in range(heads):
            to_later(h).wait_recv()
        for h in range(heads):
            moved = dot_nt(reach[h], far_maps[core, h])
            moved = moved[:tok] + moved[tok:]
            reach[h, :tok], reach[h, tok:] = split2(moved[:, :DK])
            loc[h] += moved[:, DK:]

    @pl.when((pair == 0) & (late == 0))
    def _():
        sin[...] = jnp.zeros_like(sin)

    loads[6].wait()
    loads[7].wait()

    def read(lo, hi):
        for h in range(lo, hi):
            at_home = middle & (late == 1 - h % 2) & (core == 1)

            @pl.when(jnp.logical_not(at_home | ((pair == 0) & (late == 0))))
            def _():
                first_state(h).wait_recv()

        for h in range(lo, hi):
            seen = dot_nt(reach[h], sin[h])
            att = loc[h] + (seen[:tok] + seen[tok:])
            inv = lax.rsqrt(jnp.mean(att * att, axis=-1, keepdims=True) + 1e-05)
            nrm[h] = (att * inv * gain_ref[:, h * DV : (h + 1) * DV]).astype(BF16)
        for h in range(lo, hi):
            cross(h).start()

    def mine(h):
        return nrm[h, pl.ds(pl.multiple_of(core * half, half), half), :]

    def theirs(lo, hi):
        for h in range(lo, hi):
            cross(h).wait_recv()
        return dot(jnp.concatenate([nrm_oth[h] for h in range(lo, hi)], axis=1), w_oth[lo * DV : hi * DV])

    cut = heads // 2
    read(0, cut)
    read(cut, heads)
    acc[...] = dot(jnp.concatenate([mine(h) for h in range(heads)], axis=1), w_own[...])
    weights.wait_recv()
    acc[...] += theirs(0, cut)
    out_ref[...] = (acc[...] + theirs(cut, heads)).astype(BF16)

    for h in range(heads):
        cross(h).wait_send()
    weights.wait_send()
    for h in range(heads):
        to_home(h, lambda copy: copy.wait_send())

    @pl.when((pair == 0) & (late == 0))
    def _():
        for h in range(heads):
            first_state(h).wait_send()

    @pl.when((pair == last_pair) & (late == 0))
    def _():
        for h in range(heads):
            to_later(h).wait_send()

    for group, home in homes:

        @pl.when(home)
        def _():
            for h in group:
                for c in (1, 0):
                    leave(c, h, lambda copy: copy.wait_send())

        @pl.when(home & (pair > 0))
        def _():
            for h in group:
                to_sibling(h).wait_send()
                for c in (1, 0):
                    to_partner(c, h).wait_send()


def shards(queries, key_rows, value_rows, strengths, log_gate, keep_flag, norm_gain, out_weight):
    tok = queries.shape[0]
    heads = strengths.shape[0]
    size = 2 * tok
    wide = out_weight.shape[1]
    hbm = pl.BlockSpec(memory_space=pltpu.HBM)
    vmem = pl.BlockSpec(memory_space=pltpu.VMEM)
    dma = pltpu.SemaphoreType.DMA
    operands = (
        queries, key_rows, value_rows, strengths, log_gate, keep_flag[None, :], norm_gain[None, :], out_weight,
    )
    return pl.pallas_call(
        functools.partial(pair_kernel, heads),
        out_shape=jax.ShapeDtypeStruct((tok // 2, wide), BF16),
        in_specs=[hbm] * len(operands),
        out_specs=vmem,
        scratch_shapes=[
            pltpu.VMEM(key_rows.shape, BF16),
            pltpu.VMEM(value_rows.shape, BF16),
            pltpu.VMEM((size, heads * DK), BF16),
            pltpu.VMEM(queries.shape, BF16),
            pltpu.VMEM(strengths.shape, F32),
            pltpu.VMEM(log_gate.shape, F32),
            pltpu.VMEM((1, tok), jnp.int32),
            pltpu.VMEM((1, heads * DV), F32),
            pltpu.VMEM(out_weight.shape, BF16),
            pltpu.VMEM(out_weight.shape, BF16),
            pltpu.VMEM((16, size), F32),
            pltpu.VMEM((heads, DK, size), BF16),
            pltpu.VMEM((heads, DV, size), BF16),
            pltpu.VMEM((heads, size, size), BF16),
            pltpu.VMEM((heads, size, size), BF16),
            pltpu.VMEM((heads, tok, size), F32),
            pltpu.VMEM((heads, tok, tok), F32),
            pltpu.VMEM((heads, size, size), BF16),
            pltpu.VMEM((heads, DK + DV, size), BF16),
            pltpu.VMEM((heads, DK + DV, size), BF16),
            pltpu.VMEM((heads, size, DK), BF16),
            pltpu.VMEM((heads, DK + DV, DK), BF16),
            pltpu.VMEM((heads, DV, DK), F32),
            pltpu.VMEM((heads, DK + DV, DK), BF16),
            pltpu.VMEM((2, heads, DK + DV, DK), BF16),
            pltpu.VMEM((2, heads, DK, DK), BF16),
            pltpu.VMEM((2, heads, DV, DK), F32),
            pltpu.VMEM((2, heads, DV, DK), BF16),
            pltpu.VMEM((heads, DV, DK), BF16),
            pltpu.VMEM((2, heads, DV, DK), BF16),
            pltpu.VMEM((2, heads, DV, DK), BF16),
            pltpu.VMEM((heads, 2 * tok, DK), BF16),
            pltpu.VMEM((heads, tok, DV), F32),
            pltpu.VMEM((heads, tok, DV), BF16),
            pltpu.VMEM((heads, tok // 2, DV), BF16),
            pltpu.VMEM((tok // 2, wide), F32),
            dma((len(operands),)),
            dma((heads,)),
            dma((heads,)),
            dma((2 * heads,)),
            dma((heads,)),
            dma((2 * heads,)),
            dma((4 * heads,)),
            dma((2 * heads,)),
            dma((heads,)),
            dma((heads,)),
            dma((heads,)),
            dma(()),
            dma(()),
        ],
        compiler_params=pltpu.CompilerParams(vmem_limit_bytes=28 << 20, collective_id=0, has_side_effects=True),
        name="pair_project",
    )(*(pltpu.with_memory_space_constraint(x, pltpu.HBM) for x in operands))


def solution(mesh):
    in_specs = (
        P(("groups", "seq"), "head"),
        P(("groups", "seq"), None, "head"),
        P(("groups", "seq"), None, "head"),
        P("head", None, ("groups", "seq")),
        P("head", ("groups", "seq")),
        P(("groups", "seq")),
        P("head"),
        P("head", None),
    )
    out_specs = P(("groups", "seq", "head"), None)
    return jax.shard_map(shards, mesh=mesh, in_specs=in_specs, out_specs=out_specs, check_vma=False)
```

```python
import functools

import jax
import jax.numpy as jnp
from jax import lax
from jax.experimental import pallas as pl
from jax.experimental.pallas import tpu as pltpu
from jax.sharding import PartitionSpec as P

DK = 128
DV = 128
F32 = jnp.float32
BF16 = jnp.bfloat16
MESH = pl.DeviceIdType.MESH


def split2(x):
    hi = x.astype(BF16)
    return hi, (x - hi.astype(F32)).astype(BF16)


def split3(x):
    a = x.astype(BF16)
    rest = x - a.astype(F32)
    b = rest.astype(BF16)
    return a, b, (rest - b.astype(F32)).astype(BF16)


def dot(a, b):
    return jnp.dot(a, b, preferred_element_type=F32)


def dot_nt(a, b):
    return lax.dot_general(a, b, (((1,), (1,)), ((), ())), preferred_element_type=F32)


def iotas(rows, cols):
    return lax.broadcasted_iota(jnp.int32, (rows, cols), 0), lax.broadcasted_iota(jnp.int32, (rows, cols), 1)


def pair_kernel(
    heads, q_hbm, k_hbm, v_hbm, str_hbm, log_hbm, keep_hbm, gain_hbm, w_hbm, out_ref,
    k_raw, v_raw, k_ref, q_ref, str_ref, log_ref, keep_ref, gain_ref, w_own, w_oth,
    small, kt, vt, a_hi, a_lo, c_top, c_low, xt, w0, res, xk, maps, bias, near_maps, far_maps, pmap, pbias, cin, sin, sout, smid,
    reach, loc, nrm, nrm_oth, acc,
    load_sem, map_send, near_recv, far_recv, mid_send, far_send, out_send, cin_recv, sin_recv,
    nrm_send, nrm_recv, w_send, w_recv,
):
    tok = q_ref.shape[0]
    size = 2 * tok
    n = lax.axis_size("seq")
    me = lax.axis_index("seq")
    core = lax.axis_index("head")
    sibling = 1 - core
    late = lax.rem(me, 2)
    pair = me // 2
    last_pair = n // 2 - 1
    partner = me + 1 - 2 * late
    near = lax.rem(me + 2, n)
    evens, odds = range(0, heads, 2), range(1, heads, 2)
    inside = pair < last_pair
    middle = inside & (pair > 0)
    homes = ((evens, inside & (late == 1) & (core == 1)), (odds, inside & (late == 0) & (core == 1)))

    pairs = (
        (str_hbm, str_ref),
        (log_hbm, log_ref),
        (keep_hbm, keep_ref),
        (k_hbm, k_raw),
        (v_hbm, v_raw),
        (q_hbm, q_ref),
        (gain_hbm, gain_ref),
        (w_hbm, w_own),
    )
    loads = [pltpu.make_async_copy(a, b, load_sem.at[i]) for i, (a, b) in enumerate(pairs)]
    for load in loads[:7]:
        load.start()

    barrier = pltpu.get_barrier_semaphore()

    def signal(where):
        pl.semaphore_signal(barrier, inc=1, device_id=where, device_id_type=MESH)

    signal({"head": sibling})
    for c in range(2):
        signal({"seq": partner, "head": c})

    @pl.when((pair < last_pair - 1) & (core == 1))
    def _():
        signal({"seq": near, "head": 1})

    @pl.when((pair == last_pair - 1) & (core == 1))
    def _():
        for c in range(2):
            signal({"seq": near, "head": c})
            signal({"seq": lax.rem(me + 3 - 2 * late, n), "head": c})

    @pl.when(middle & (core == 1))
    def _():
        signal({"seq": me - 2, "head": 1})

    @pl.when((pair == last_pair) & (pair > 0))
    def _():
        signal({"seq": me - 2, "head": 1})
        signal({"seq": me - 1 - 2 * late, "head": 1})

    peers = (
        3
        + jnp.where((pair < last_pair - 1) & (core == 1), 1, 0)
        + jnp.where((pair == last_pair - 1) & (core == 1), 4, 0)
        + jnp.where(middle & (core == 1), 1, 0)
        + jnp.where((pair == last_pair) & (pair > 0), 2, 0)
    )

    def remote(src, dst, ssem, rsem, where):
        return pltpu.make_async_remote_copy(
            src_ref=src, dst_ref=dst, send_sem=ssem, recv_sem=rsem, device_id=where, device_id_type=MESH
        )

    def flat(c, h):
        return c * heads + h

    def whole(make, act, earlier):
        if earlier:

            @pl.when(pair == 0)
            def _():
                act(make(pl.ds(DK, DV)))

            @pl.when(pair > 0)
            def _():
                act(make(pl.ds(0, DK + DV)))

        else:
            act(make(pl.ds(0, DK + DV)))

    def over(h):
        return lambda span: remote(
            maps.at[h, span], near_maps.at[h, span], map_send.at[h], near_recv.at[h], {"head": 1}
        )

    def across(c, h):
        return lambda span: remote(
            maps.at[h, span], far_maps.at[c, h, span], map_send.at[h], far_recv.at[flat(c, h)],
            {"seq": partner, "head": 1},
        )

    def to_home(h, act):
        earlier = 1 if h % 2 == 0 else 0

        @pl.when(inside & (late != earlier))
        def _():
            whole(across(core, h), act, h % 2 == 0)

        @pl.when(inside & (late == earlier) & (core == 0))
        def _():
            whole(over(h), act, h % 2 == 1)

    def to_later(h):
        return remote(
            maps.at[h], far_maps.at[core, h], map_send.at[h], far_recv.at[flat(core, h)], {"seq": partner}
        )

    def first_state(h):
        return remote(maps.at[h, pl.ds(DK, DV)], sin.at[h], mid_send.at[h], sin_recv.at[h], {"seq": partner})

    def leave(c, h, act):
        @pl.when(pair == last_pair - 1)
        def _():
            for k, target in enumerate((lax.rem(me + 3 - 2 * late, n), near)):
                act(
                    remote(
                        sout.at[c, h], sin.at[h], out_send.at[2 * flat(c, h) + k], sin_recv.at[h],
                        {"seq": target, "head": c},
                    )
                )

        @pl.when(pair < last_pair - 1)
        def _():
            act(enter(c, h))

    def enter(c, h):
        return remote(
            sout.at[c, h], cin.at[c, h], out_send.at[2 * flat(c, h)], cin_recv.at[flat(c, h)],
            {"seq": near, "head": 1},
        )

    def to_sibling(h):
        src = smid.at[0, h] if h % 2 == 0 else cin.at[0, h]
        return remote(src, sin.at[h], mid_send.at[h], sin_recv.at[h], {"head": 0})

    def to_partner(c, h):
        src = cin.at[c, h] if h % 2 == 0 else smid.at[c, h]
        return remote(src, sin.at[h], far_send.at[flat(c, h)], sin_recv.at[h], {"seq": partner, "head": c})

    half = tok // 2

    def cross(h):
        span = pl.ds(pl.multiple_of(sibling * half, half), half)
        return remote(nrm.at[h, span], nrm_oth.at[h], nrm_send.at[h], nrm_recv.at[h], {"head": sibling})

    weights = remote(w_hbm, w_oth, w_send, w_recv, {"head": sibling})

    for load in loads[:3]:
        load.wait()
    live = keep_ref[...].astype(F32)
    small[...] = jnp.zeros_like(small)
    small[:heads, :tok] = str_ref[:, 0, :] * live
    small[:heads, tok:] = str_ref[:, 1, :] * live
    small[8 : 8 + heads, :tok] = log_ref[...] * live
    r_i, c_i = iotas(size, size)
    place = jnp.where(jnp.where(r_i < tok, 2 * r_i, 2 * (r_i - tok) + 1) == c_i, 1.0, 0.0).astype(BF16)
    r_t, c_t = iotas(tok, size)
    upto = jnp.where(2 * r_t <= c_t, 1.0, 0.0).astype(BF16)
    r_c, c_c = iotas(size, tok)
    upto_c = jnp.where(2 * c_c <= r_c, 1.0, 0.0).astype(BF16)
    s3 = split3(small[...])
    beta_rows = dot(s3[0][:8], place) + (dot(s3[1][:8], place) + dot(s3[2][:8], place))
    logs = [s[8:, :tok] for s in s3]
    cum_rows = dot(logs[0], upto) + (dot(logs[1], upto) + dot(logs[2], upto))
    cum_cols = dot_nt(upto_c, logs[0]) + (dot_nt(upto_c, logs[1]) + dot_nt(upto_c, logs[2]))

    loads[3].wait()
    loads[7].start()
    k_ref[...] = k_raw[...].reshape(k_ref.shape)
    row_t, col_t = iotas(tok, tok)
    after = col_t > row_t
    after_top = c_t > r_t
    eye = jnp.where(row_t == col_t, 1.0, 0.0)
    betas, cums, squares = [], [], []
    for h in range(heads):
        span = slice(h * DK, (h + 1) * DK)
        kt[h] = k_ref[:, span].T
        ktf = kt[h].astype(F32)
        ss = jnp.sum(ktf * ktf, axis=0, keepdims=True) + 1e-06
        beta = beta_rows[h : h + 1]
        cum = cum_rows[h : h + 1]
        betas.append(beta)
        cums.append(cum)
        squares.append(ss)
        scale = beta / ss
        cum_col = cum_cols[:, h : h + 1]
        top = (scale * jnp.exp(jnp.minimum(cum - cum_col[:tok], 0.0))) * dot(k_ref[:tok, span], kt[h])
        low = (scale[:, tok:] * jnp.exp(jnp.minimum(cum[:, tok:] - cum_col[tok:], 0.0))) * dot(
            k_ref[tok:, span], kt[h, :, tok:]
        )
        top = jnp.where(after_top, top, 0.0)
        low = jnp.where(after, low, 0.0)
        c_top[h] = top
        c_low[h] = low
        a_hi[h, :tok], a_lo[h, :tok] = split2(top)
        a_hi[h, tok:, tok:], a_lo[h, tok:, tok:] = split2(low)
        zero = jnp.zeros((tok, tok), BF16)
        a_hi[h, tok:, :tok] = zero
        a_lo[h, tok:, :tok] = zero
        xt[h, tok:, :tok] = zero

    pl.semaphore_wait(barrier, peers)
    weights.start()

    eye_b = eye.astype(BF16)
    steps = tok.bit_length() - 1
    for bit in range(steps):
        step = 1 << bit
        spans = [slice(0, tok)] if step < 16 else [slice(at, at + step) for at in range(0, tok, 2 * step)]

        def take(ref_rows):
            return jnp.concatenate([ref_rows(span) for span in spans], axis=0)

        low_bit = take(lambda span: row_t[span]) >> bit
        picked = ((take(lambda span: col_t[span]) >> bit) == (low_bit | 1)) & ((low_bit & 1) == 0)
        for h in range(heads):
            for c_ref, at in ((c_top, 0), (c_low, tok)):
                own = slice(at, at + tok)
                side = c_ref.shape[2]
                m = jnp.where(picked, take(lambda span: c_ref[h, span, :tok]), 0.0).astype(BF16)
                first = 0 if bit + 1 < steps else tok
                x = eye_b if bit == 0 else xt[h, own, own]
                if step < 16:
                    c_hi, c_lo = split2(c_ref[h])
                    if bit > 0:
                        c_hi = jnp.concatenate([c_hi, x], axis=1)
                        c_lo = jnp.concatenate([c_lo, jnp.zeros_like(x)], axis=1)
                    moved = dot(jnp.concatenate([m, m], axis=1), jnp.concatenate([c_hi, c_lo], axis=0))
                elif side > first:
                    moved = dot(m, jnp.concatenate([c_ref[h, :, first:].astype(BF16), x], axis=1))
                else:
                    moved = dot(m, x)
                if bit == 0:
                    xt[h, own, own] = x
                done = 0
                for span in spans:
                    count = span.stop - span.start
                    part = slice(done, done + count)
                    if side > first:
                        c_ref[h, span, first:] -= moved[part, : side - first]
                    gone = m[part] if bit == 0 else moved[part, side - first :].astype(BF16)
                    rows_at = slice(at + span.start, at + span.stop)
                    xt[h, rows_at, own] = x[span] - gone
                    done += count
    for h in range(heads):
        xt[h, :tok, tok:] = -dot(c_top[h, :, tok:].astype(BF16), xt[h, tok:, tok:]).astype(BF16)

    loads[4].wait()
    v_flat = v_raw[...].reshape(k_ref.shape)
    for h in range(heads):
        vt[h] = v_flat[:, h * DV : (h + 1) * DV].T

    for group in (odds, evens):
        rhs, fade = {}, {}
        for h in group:
            beta, cum, ss = betas[h], cums[h], squares[h]
            rhs[h] = jnp.concatenate(
                [(beta * jnp.exp(cum) / ss) * kt[h].astype(F32), (beta * lax.rsqrt(ss)) * vt[h].astype(F32)], axis=0
            )
            fade[h] = jnp.exp(cum[:, size - 1 : size] - cum)
        for h in group:
            w0[h] = dot(rhs[h].astype(BF16), xt[h]).astype(BF16)
        for h in group:
            keys = k_ref[:, h * DK : (h + 1) * DK]
            xk[h] = dot((xt[h].astype(F32) * fade[h]).astype(BF16), keys).astype(BF16)
        for h in group:
            twice = jnp.concatenate([w0[h], w0[h]], axis=1)
            res[h] = (rhs[h] - w0[h].astype(F32) - dot(twice, jnp.concatenate([a_hi[h], a_lo[h]], axis=0))).astype(BF16)
        for h in group:
            keys = k_ref[:, h * DK : (h + 1) * DK]
            faded = split2(w0[h].astype(F32) * fade[h])
            tb = dot(
                jnp.concatenate([faded[0], faded[1], res[h]], axis=1), jnp.concatenate([keys, keys, xk[h]], axis=0)
            )
            maps[h, :DK] = (eye * jnp.exp(cums[h][:, size - 1 : size]) - tb[:DK]).astype(BF16)
            maps[h, DK:] = tb[DK:].astype(BF16)
            bias[h] = tb[DK:]

        for h in group:
            to_home(h, lambda copy: copy.start())

    @pl.when((pair == 0) & (late == 0))
    def _():
        for h in range(heads):
            first_state(h).start()

    @pl.when((pair == last_pair) & (late == 0))
    def _():
        for h in range(heads):
            to_later(h).start()

    loads[5].wait()
    t_i, l_i = iotas(tok, size)
    visible = l_i <= 2 * t_i + 1
    tok_r, tok_c = iotas(tok, tok)
    upto_t = jnp.where(tok_c <= tok_r, 1.0, 0.0).astype(BF16)
    cum_toks = dot_nt(upto_t, logs[0]) + (dot_nt(upto_t, logs[1]) + dot_nt(upto_t, logs[2]))
    for h in range(heads):
        q = q_ref[:, h * DK : (h + 1) * DK]
        qf = q.astype(F32)
        rq = lax.rsqrt(jnp.sum(qf * qf, axis=-1, keepdims=True) + 1e-06)
        cum_tok = cum_toks[:, h : h + 1]
        decay = jnp.where(visible, jnp.exp(jnp.minimum(cum_tok - cums[h], 0.0)), 0.0)
        mix = split2((rq * decay) * dot(q, kt[h]))
        w = split2(w0[h].astype(F32) + dot(res[h], xt[h]))
        both = dot_nt(mix[0], w[0]) + (dot_nt(mix[0], w[1]) + dot_nt(mix[1], w[0]))
        reach[h, :tok], reach[h, tok:] = split2((jnp.exp(cum_tok) * rq) * qf - both[:, :DK])
        loc[h] = both[:, DK:]

    for group, home in homes:

        @pl.when(home)
        def _():
            for h in group:
                for c in (1, 0):
                    if c == 0:
                        whole(over(h), lambda copy: copy.wait_recv(), h % 2 == 1)
                    whole(across(c, h), lambda copy: copy.wait_recv(), h % 2 == 0)
                    own_map = maps.at[h] if c == 1 else near_maps.at[h]
                    one, two = (far_maps.at[c, h], own_map) if h % 2 == 0 else (own_map, far_maps.at[c, h])
                    exact = c == 1 and h % 2 == 0
                    trans, shift = two[:DK], bias[h] if exact else two[DK:].astype(F32)

                    @pl.when(pair == 0)
                    def _():
                        sout[c, h] = (dot(one[DK:], trans) + shift).astype(BF16)
                        leave(c, h, lambda copy: copy.start())

                    @pl.when(pair > 0)
                    def _():
                        both = dot(one[...], trans)
                        pmap[c, h] = both[:DK].astype(BF16)
                        pbias[c, h] = both[DK:] + shift

    for group, home in homes:

        @pl.when(home & (pair > 0))
        def _():
            for h in group:
                for c in (0, 1):
                    enter(c, h).wait_recv()
                    sout[c, h] = (dot(cin[c, h], pmap[c, h]) + pbias[c, h]).astype(BF16)
                    leave(c, h, lambda copy: copy.start())
                    if h % 2 == 0:
                        to_partner(c, h).start()
                    elif c == 0:
                        to_sibling(h).start()
                    else:
                        sin[h] = cin[c, h]
                for c in (0, 1):
                    if h % 2 == 0:
                        one, shift = far_maps.at[c, h], far_maps[c, h, DK:].astype(F32)
                    elif c == 1:
                        one, shift = maps.at[h], bias[h]
                    else:
                        one, shift = near_maps.at[h], near_maps[h, DK:].astype(F32)
                    smid[c, h] = (dot(cin[c, h], one[:DK]) + shift).astype(BF16)
                    if h % 2 == 1:
                        to_partner(c, h).start()
                    elif c == 0:
                        to_sibling(h).start()
                    else:
                        sin[h] = smid[c, h]

    @pl.when((late == 1) & (pair == last_pair))
    def _():
        for h in range(heads):
            to_later(h).wait_recv()
        for h in range(heads):
            moved = dot_nt(reach[h], far_maps[core, h])
            moved = moved[:tok] + moved[tok:]
            reach[h, :tok], reach[h, tok:] = split2(moved[:, :DK])
            loc[h] += moved[:, DK:]

    @pl.when((pair == 0) & (late == 0))
    def _():
        sin[...] = jnp.zeros_like(sin)

    loads[6].wait()
    loads[7].wait()

    def read(lo, hi):
        for h in range(lo, hi):
            at_home = middle & (late == 1 - h % 2) & (core == 1)

            @pl.when(jnp.logical_not(at_home | ((pair == 0) & (late == 0))))
            def _():
                first_state(h).wait_recv()

        for h in range(lo, hi):
            seen = dot_nt(reach[h], sin[h])
            att = loc[h] + (seen[:tok] + seen[tok:])
            inv = lax.rsqrt(jnp.mean(att * att, axis=-1, keepdims=True) + 1e-05)
            nrm[h] = (att * inv * gain_ref[:, h * DV : (h + 1) * DV]).astype(BF16)
        for h in range(lo, hi):
            cross(h).start()

    def mine(h):
        return nrm[h, pl.ds(pl.multiple_of(core * half, half), half), :]

    def theirs(lo, hi):
        for h in range(lo, hi):
            cross(h).wait_recv()
        return dot(jnp.concatenate([nrm_oth[h] for h in range(lo, hi)], axis=1), w_oth[lo * DV : hi * DV])

    cut = heads // 2
    read(0, cut)
    read(cut, heads)
    acc[...] = dot(jnp.concatenate([mine(h) for h in range(heads)], axis=1), w_own[...])
    weights.wait_recv()
    acc[...] += theirs(0, cut)
    out_ref[...] = (acc[...] + theirs(cut, heads)).astype(BF16)

    for h in range(heads):
        cross(h).wait_send()
    weights.wait_send()
    for h in range(heads):
        to_home(h, lambda copy: copy.wait_send())

    @pl.when((pair == 0) & (late == 0))
    def _():
        for h in range(heads):
            first_state(h).wait_send()

    @pl.when((pair == last_pair) & (late == 0))
    def _():
        for h in range(heads):
            to_later(h).wait_send()

    for group, home in homes:

        @pl.when(home)
        def _():
            for h in group:
                for c in (0, 1):
                    leave(c, h, lambda copy: copy.wait_send())

        @pl.when(home & (pair > 0))
        def _():
            for h in group:
                to_sibling(h).wait_send()
                for c in (0, 1):
                    to_partner(c, h).wait_send()


def shards(queries, key_rows, value_rows, strengths, log_gate, keep_flag, norm_gain, out_weight):
    tok = queries.shape[0]
    heads = strengths.shape[0]
    size = 2 * tok
    wide = out_weight.shape[1]
    hbm = pl.BlockSpec(memory_space=pltpu.HBM)
    vmem = pl.BlockSpec(memory_space=pltpu.VMEM)
    dma = pltpu.SemaphoreType.DMA
    operands = (
        queries, key_rows, value_rows, strengths, log_gate, keep_flag[None, :], norm_gain[None, :], out_weight,
    )
    return pl.pallas_call(
        functools.partial(pair_kernel, heads),
        out_shape=jax.ShapeDtypeStruct((tok // 2, wide), BF16),
        in_specs=[hbm] * len(operands),
        out_specs=vmem,
        scratch_shapes=[
            pltpu.VMEM(key_rows.shape, BF16),
            pltpu.VMEM(value_rows.shape, BF16),
            pltpu.VMEM((size, heads * DK), BF16),
            pltpu.VMEM(queries.shape, BF16),
            pltpu.VMEM(strengths.shape, F32),
            pltpu.VMEM(log_gate.shape, F32),
            pltpu.VMEM((1, tok), jnp.int32),
            pltpu.VMEM((1, heads * DV), F32),
            pltpu.VMEM(out_weight.shape, BF16),
            pltpu.VMEM(out_weight.shape, BF16),
            pltpu.VMEM((16, size), F32),
            pltpu.VMEM((heads, DK, size), BF16),
            pltpu.VMEM((heads, DV, size), BF16),
            pltpu.VMEM((heads, size, size), BF16),
            pltpu.VMEM((heads, size, size), BF16),
            pltpu.VMEM((heads, tok, size), F32),
            pltpu.VMEM((heads, tok, tok), F32),
            pltpu.VMEM((heads, size, size), BF16),
            pltpu.VMEM((heads, DK + DV, size), BF16),
            pltpu.VMEM((heads, DK + DV, size), BF16),
            pltpu.VMEM((heads, size, DK), BF16),
            pltpu.VMEM((heads, DK + DV, DK), BF16),
            pltpu.VMEM((heads, DV, DK), F32),
            pltpu.VMEM((heads, DK + DV, DK), BF16),
            pltpu.VMEM((2, heads, DK + DV, DK), BF16),
            pltpu.VMEM((2, heads, DK, DK), BF16),
            pltpu.VMEM((2, heads, DV, DK), F32),
            pltpu.VMEM((2, heads, DV, DK), BF16),
            pltpu.VMEM((heads, DV, DK), BF16),
            pltpu.VMEM((2, heads, DV, DK), BF16),
            pltpu.VMEM((2, heads, DV, DK), BF16),
            pltpu.VMEM((heads, 2 * tok, DK), BF16),
            pltpu.VMEM((heads, tok, DV), F32),
            pltpu.VMEM((heads, tok, DV), BF16),
            pltpu.VMEM((heads, tok // 2, DV), BF16),
            pltpu.VMEM((tok // 2, wide), F32),
            dma((len(operands),)),
            dma((heads,)),
            dma((heads,)),
            dma((2 * heads,)),
            dma((heads,)),
            dma((2 * heads,)),
            dma((4 * heads,)),
            dma((2 * heads,)),
            dma((heads,)),
            dma((heads,)),
            dma((heads,)),
            dma(()),
            dma(()),
        ],
        compiler_params=pltpu.CompilerParams(vmem_limit_bytes=28 << 20, collective_id=0, has_side_effects=True),
        name="pair_project",
    )(*(pltpu.with_memory_space_constraint(x, pltpu.HBM) for x in operands))


def solution(mesh):
    in_specs = (
        P(("groups", "seq"), "head"),
        P(("groups", "seq"), None, "head"),
        P(("groups", "seq"), None, "head"),
        P("head", None, ("groups", "seq")),
        P("head", ("groups", "seq")),
        P(("groups", "seq")),
        P("head"),
        P("head", None),
    )
    out_specs = P(("groups", "seq", "head"), None)
    return jax.shard_map(shards, mesh=mesh, in_specs=in_specs, out_specs=out_specs, check_vma=False)
```

```python
import functools

import jax
import jax.numpy as jnp
from jax import lax
from jax.experimental import pallas as pl
from jax.experimental.pallas import tpu as pltpu
from jax.sharding import PartitionSpec as P

DK = 128
DV = 128
F32 = jnp.float32
BF16 = jnp.bfloat16
MESH = pl.DeviceIdType.MESH


def split2(x):
    hi = x.astype(BF16)
    return hi, (x - hi.astype(F32)).astype(BF16)


def split3(x):
    a = x.astype(BF16)
    rest = x - a.astype(F32)
    b = rest.astype(BF16)
    return a, b, (rest - b.astype(F32)).astype(BF16)


def dot(a, b):
    return jnp.dot(a, b, preferred_element_type=F32)


def dot_nt(a, b):
    return lax.dot_general(a, b, (((1,), (1,)), ((), ())), preferred_element_type=F32)


def iotas(rows, cols):
    return lax.broadcasted_iota(jnp.int32, (rows, cols), 0), lax.broadcasted_iota(jnp.int32, (rows, cols), 1)


def pair_kernel(
    heads, q_hbm, k_hbm, v_hbm, str_hbm, log_hbm, keep_hbm, gain_hbm, w_hbm, out_ref,
    k_raw, v_raw, k_ref, q_ref, str_ref, log_ref, keep_ref, gain_ref, w_own, w_oth,
    small, kt, vt, a_hi, a_lo, c_top, c_low, xt, w0, res, xk, maps, bias, near_maps, far_maps, pmap, pbias, cin, sin, sout, smid,
    reach, loc, nrm, nrm_oth, acc,
    load_sem, map_send, near_recv, far_recv, mid_send, far_send, out_send, cin_recv, sin_recv,
    nrm_send, nrm_recv, w_send, w_recv,
):
    tok = q_ref.shape[0]
    size = 2 * tok
    n = lax.axis_size("seq")
    me = lax.axis_index("seq")
    core = lax.axis_index("head")
    sibling = 1 - core
    late = lax.rem(me, 2)
    pair = me // 2
    last_pair = n // 2 - 1
    partner = me + 1 - 2 * late
    near = lax.rem(me + 2, n)
    evens, odds = range(0, heads, 2), range(1, heads, 2)
    inside = pair < last_pair
    middle = inside & (pair > 0)
    homes = ((evens, inside & (late == 1) & (core == 1)), (odds, inside & (late == 0) & (core == 1)))

    pairs = (
        (str_hbm, str_ref),
        (log_hbm, log_ref),
        (keep_hbm, keep_ref),
        (k_hbm, k_raw),
        (v_hbm, v_raw),
        (q_hbm, q_ref),
        (gain_hbm, gain_ref),
        (w_hbm, w_own),
    )
    loads = [pltpu.make_async_copy(a, b, load_sem.at[i]) for i, (a, b) in enumerate(pairs)]
    for load in loads[:7]:
        load.start()

    barrier = pltpu.get_barrier_semaphore()

    def signal(where):
        pl.semaphore_signal(barrier, inc=1, device_id=where, device_id_type=MESH)

    signal({"head": sibling})
    for c in range(2):
        signal({"seq": partner, "head": c})

    @pl.when((pair < last_pair - 1) & (core == 1))
    def _():
        signal({"seq": near, "head": 1})

    @pl.when((pair == last_pair - 1) & (core == 1))
    def _():
        for c in range(2):
            signal({"seq": near, "head": c})
            signal({"seq": lax.rem(me + 3 - 2 * late, n), "head": c})

    @pl.when(middle & (core == 1))
    def _():
        signal({"seq": me - 2, "head": 1})

    @pl.when((pair == last_pair) & (pair > 0))
    def _():
        signal({"seq": me - 2, "head": 1})
        signal({"seq": me - 1 - 2 * late, "head": 1})

    peers = (
        3
        + jnp.where((pair < last_pair - 1) & (core == 1), 1, 0)
        + jnp.where((pair == last_pair - 1) & (core == 1), 4, 0)
        + jnp.where(middle & (core == 1), 1, 0)
        + jnp.where((pair == last_pair) & (pair > 0), 2, 0)
    )

    def remote(src, dst, ssem, rsem, where):
        return pltpu.make_async_remote_copy(
            src_ref=src, dst_ref=dst, send_sem=ssem, recv_sem=rsem, device_id=where, device_id_type=MESH
        )

    def flat(c, h):
        return c * heads + h

    every, bias_only = pl.ds(0, DK + DV), pl.ds(DK, DV)

    def over(h):
        return lambda span: remote(
            maps.at[h, span], near_maps.at[h, span], map_send.at[h], near_recv.at[h], {"head": 1}
        )

    def across(c, h):
        return lambda span: remote(
            maps.at[h, span], far_maps.at[c, h, span], map_send.at[h], far_recv.at[flat(c, h)],
            {"seq": partner, "head": 1},
        )

    def to_homes(group, act):
        home_late = 0 if group is odds else 1
        start = inside & (pair == 0) & (late == 0)
        later = inside & jnp.logical_not((pair == 0) & (late == 0))
        for case, span in ((start, bias_only), (later, every)):

            @pl.when(case & (late != home_late))
            def _():
                for h in group:
                    act(across(core, h)(span))

            @pl.when(case & (late == home_late) & (core == 0))
            def _():
                for h in group:
                    act(over(h)(span))

    def to_later(h):
        return remote(
            maps.at[h], far_maps.at[core, h], map_send.at[h], far_recv.at[flat(core, h)], {"seq": partner}
        )

    def first_state(h):
        return remote(maps.at[h, pl.ds(DK, DV)], sin.at[h], mid_send.at[h], sin_recv.at[h], {"seq": partner})

    def leave(c, h, to_readers):
        if not to_readers:
            return [enter(c, h)]
        return [
            remote(
                sout.at[c, h], sin.at[h], out_send.at[2 * flat(c, h) + k], sin_recv.at[h], {"seq": target, "head": c}
            )
            for k, target in enumerate((lax.rem(me + 3 - 2 * late, n), near))
        ]

    def enter(c, h):
        return remote(
            sout.at[c, h], cin.at[c, h], out_send.at[2 * flat(c, h)], cin_recv.at[flat(c, h)],
            {"seq": near, "head": 1},
        )

    def to_sibling(h):
        src = smid.at[0, h] if h % 2 == 0 else cin.at[0, h]
        return remote(src, sin.at[h], mid_send.at[h], sin_recv.at[h], {"head": 0})

    def to_partner(c, h):
        src = cin.at[c, h] if h % 2 == 0 else smid.at[c, h]
        return remote(src, sin.at[h], far_send.at[flat(c, h)], sin_recv.at[h], {"seq": partner, "head": c})

    half = tok // 2

    def cross(h):
        span = pl.ds(pl.multiple_of(sibling * half, half), half)
        return remote(nrm.at[h, span], nrm_oth.at[h], nrm_send.at[h], nrm_recv.at[h], {"head": sibling})

    weights = remote(w_hbm, w_oth, w_send, w_recv, {"head": sibling})

    for load in loads[:3]:
        load.wait()
    live = keep_ref[...].astype(F32)
    small[...] = jnp.zeros_like(small)
    small[:heads, :tok] = str_ref[:, 0, :] * live
    small[:heads, tok:] = str_ref[:, 1, :] * live
    small[8 : 8 + heads, :tok] = log_ref[...] * live
    r_i, c_i = iotas(size, size)
    place = jnp.where(jnp.where(r_i < tok, 2 * r_i, 2 * (r_i - tok) + 1) == c_i, 1.0, 0.0).astype(BF16)
    r_t, c_t = iotas(tok, size)
    upto = jnp.where(2 * r_t <= c_t, 1.0, 0.0).astype(BF16)
    r_c, c_c = iotas(size, tok)
    upto_c = jnp.where(2 * c_c <= r_c, 1.0, 0.0).astype(BF16)
    s3 = split3(small[...])
    beta_rows = dot(s3[0][:8], place) + (dot(s3[1][:8], place) + dot(s3[2][:8], place))
    logs = [s[8:, :tok] for s in s3]
    cum_rows = dot(logs[0], upto) + (dot(logs[1], upto) + dot(logs[2], upto))
    cum_cols = dot_nt(upto_c, logs[0]) + (dot_nt(upto_c, logs[1]) + dot_nt(upto_c, logs[2]))

    loads[3].wait()
    loads[7].start()
    k_ref[...] = k_raw[...].reshape(k_ref.shape)
    row_t, col_t = iotas(tok, tok)
    after = col_t > row_t
    after_top = c_t > r_t
    eye = jnp.where(row_t == col_t, 1.0, 0.0)
    betas, cums, squares = [], [], []
    for h in range(heads):
        span = slice(h * DK, (h + 1) * DK)
        kt[h] = k_ref[:, span].T
        ktf = kt[h].astype(F32)
        ss = jnp.sum(ktf * ktf, axis=0, keepdims=True) + 1e-06
        beta = beta_rows[h : h + 1]
        cum = cum_rows[h : h + 1]
        betas.append(beta)
        cums.append(cum)
        squares.append(ss)
        scale = beta / ss
        cum_col = cum_cols[:, h : h + 1]
        top = (scale * jnp.exp(jnp.minimum(cum - cum_col[:tok], 0.0))) * dot(k_ref[:tok, span], kt[h])
        low = (scale[:, tok:] * jnp.exp(jnp.minimum(cum[:, tok:] - cum_col[tok:], 0.0))) * dot(
            k_ref[tok:, span], kt[h, :, tok:]
        )
        top = jnp.where(after_top, top, 0.0)
        low = jnp.where(after, low, 0.0)
        c_top[h] = top
        c_low[h] = low
        a_hi[h, :tok], a_lo[h, :tok] = split2(top)
        a_hi[h, tok:, tok:], a_lo[h, tok:, tok:] = split2(low)
        zero = jnp.zeros((tok, tok), BF16)
        a_hi[h, tok:, :tok] = zero
        a_lo[h, tok:, :tok] = zero
        xt[h, tok:, :tok] = zero


    eye_b = eye.astype(BF16)
    steps = tok.bit_length() - 1
    for bit in range(steps):
        step = 1 << bit
        spans = [slice(0, tok)] if step < 16 else [slice(at, at + step) for at in range(0, tok, 2 * step)]

        def take(ref_rows):
            return jnp.concatenate([ref_rows(span) for span in spans], axis=0)

        low_bit = take(lambda span: row_t[span]) >> bit
        picked = ((take(lambda span: col_t[span]) >> bit) == (low_bit | 1)) & ((low_bit & 1) == 0)
        for h in range(heads):
            for c_ref, at in ((c_top, 0), (c_low, tok)):
                own = slice(at, at + tok)
                side = c_ref.shape[2]
                m = jnp.where(picked, take(lambda span: c_ref[h, span, :tok]), 0.0).astype(BF16)
                first = 0 if bit + 1 < steps else tok
                x = eye_b if bit == 0 else xt[h, own, own]
                if step < 16:
                    c_hi, c_lo = split2(c_ref[h])
                    if bit > 0:
                        c_hi = jnp.concatenate([c_hi, x], axis=1)
                        c_lo = jnp.concatenate([c_lo, jnp.zeros_like(x)], axis=1)
                    moved = dot(jnp.concatenate([m, m], axis=1), jnp.concatenate([c_hi, c_lo], axis=0))
                elif side > first:
                    moved = dot(m, jnp.concatenate([c_ref[h, :, first:].astype(BF16), x], axis=1))
                else:
                    moved = dot(m, x)
                if bit == 0:
                    xt[h, own, own] = x
                done = 0
                for span in spans:
                    count = span.stop - span.start
                    part = slice(done, done + count)
                    if side > first:
                        c_ref[h, span, first:] -= moved[part, : side - first]
                    gone = m[part] if bit == 0 else moved[part, side - first :].astype(BF16)
                    rows_at = slice(at + span.start, at + span.stop)
                    xt[h, rows_at, own] = x[span] - gone
                    done += count
    for h in range(heads):
        xt[h, :tok, tok:] = -dot(c_top[h, :, tok:].astype(BF16), xt[h, tok:, tok:]).astype(BF16)

    pl.semaphore_wait(barrier, peers)
    weights.start()
    loads[4].wait()
    v_flat = v_raw[...].reshape(k_ref.shape)
    for h in range(heads):
        vt[h] = v_flat[:, h * DV : (h + 1) * DV].T

    for group in (odds, evens):
        rhs, fade = {}, {}
        for h in group:
            beta, cum, ss = betas[h], cums[h], squares[h]
            rhs[h] = jnp.concatenate(
                [(beta * jnp.exp(cum) / ss) * kt[h].astype(F32), (beta * lax.rsqrt(ss)) * vt[h].astype(F32)], axis=0
            )
            fade[h] = jnp.exp(cum[:, size - 1 : size] - cum)
        for h in group:
            w0[h] = dot(rhs[h].astype(BF16), xt[h]).astype(BF16)
        for h in group:
            keys = k_ref[:, h * DK : (h + 1) * DK]
            xk[h] = dot((xt[h].astype(F32) * fade[h]).astype(BF16), keys).astype(BF16)
        for h in group:
            twice = jnp.concatenate([w0[h], w0[h]], axis=1)
            res[h] = (rhs[h] - w0[h].astype(F32) - dot(twice, jnp.concatenate([a_hi[h], a_lo[h]], axis=0))).astype(BF16)
        for h in group:
            keys = k_ref[:, h * DK : (h + 1) * DK]
            faded = split2(w0[h].astype(F32) * fade[h])
            tb = dot(
                jnp.concatenate([faded[0], faded[1], res[h]], axis=1), jnp.concatenate([keys, keys, xk[h]], axis=0)
            )
            maps[h, :DK] = (eye * jnp.exp(cums[h][:, size - 1 : size]) - tb[:DK]).astype(BF16)
            maps[h, DK:] = tb[DK:].astype(BF16)
            bias[h] = tb[DK:]

        to_homes(group, lambda copy: copy.start())

    @pl.when((pair == 0) & (late == 0))
    def _():
        for h in range(heads):
            first_state(h).start()

    @pl.when((pair == last_pair) & (late == 0))
    def _():
        for h in range(heads):
            to_later(h).start()

    loads[5].wait()
    t_i, l_i = iotas(tok, size)
    visible = l_i <= 2 * t_i + 1
    tok_r, tok_c = iotas(tok, tok)
    upto_t = jnp.where(tok_c <= tok_r, 1.0, 0.0).astype(BF16)
    cum_toks = dot_nt(upto_t, logs[0]) + (dot_nt(upto_t, logs[1]) + dot_nt(upto_t, logs[2]))
    for h in range(heads):
        q = q_ref[:, h * DK : (h + 1) * DK]
        qf = q.astype(F32)
        rq = lax.rsqrt(jnp.sum(qf * qf, axis=-1, keepdims=True) + 1e-06)
        cum_tok = cum_toks[:, h : h + 1]
        decay = jnp.where(visible, jnp.exp(jnp.minimum(cum_tok - cums[h], 0.0)), 0.0)
        mix = split2((rq * decay) * dot(q, kt[h]))
        w = split2(w0[h].astype(F32) + dot(res[h], xt[h]))
        both = dot_nt(mix[0], w[0]) + (dot_nt(mix[0], w[1]) + dot_nt(mix[1], w[0]))
        reach[h, :tok], reach[h, tok:] = split2((jnp.exp(cum_tok) * rq) * qf - both[:, :DK])
        loc[h] = both[:, DK:]

    def arrive(c, h, first):
        own_map = maps.at[h] if c == 1 else near_maps.at[h]
        if c == 0:
            over(h)(bias_only if first and h % 2 == 1 else every).wait_recv()
        across(c, h)(bias_only if first and h % 2 == 0 else every).wait_recv()
        one, two = (far_maps.at[c, h], own_map) if h % 2 == 0 else (own_map, far_maps.at[c, h])
        exact = c == 1 and h % 2 == 0
        return one, two[:DK], bias[h] if exact else two[DK:].astype(F32)

    def pass_on(c, h, to_readers):
        enter(c, h).wait_recv()
        sout[c, h] = (dot(cin[c, h], pmap[c, h]) + pbias[c, h]).astype(BF16)
        for copy in leave(c, h, to_readers):
            copy.start()
        if h % 2 == 0:
            to_partner(c, h).start()
        elif c == 0:
            to_sibling(h).start()
        else:
            sin[h] = cin[c, h]

    def between(c, h):
        if h % 2 == 0:
            one, shift = far_maps.at[c, h], far_maps[c, h, DK:].astype(F32)
        elif c == 1:
            one, shift = maps.at[h], bias[h]
        else:
            one, shift = near_maps.at[h], near_maps[h, DK:].astype(F32)
        smid[c, h] = (dot(cin[c, h], one[:DK]) + shift).astype(BF16)
        if h % 2 == 1:
            to_partner(c, h).start()
        elif c == 0:
            to_sibling(h).start()
        else:
            sin[h] = smid[c, h]

    for group, home in homes:

        @pl.when(home & (pair == 0))
        def _():
            for h in group:
                for c in (1, 0):
                    one, trans, shift = arrive(c, h, True)
                    sout[c, h] = (dot(one[DK:], trans) + shift).astype(BF16)
                    for copy in leave(c, h, last_pair == 1):
                        copy.start()

        @pl.when(home & (pair > 0))
        def _():
            for h in group:
                for c in (1, 0):
                    one, trans, shift = arrive(c, h, False)
                    both = dot(one[...], trans)
                    pmap[c, h] = both[:DK].astype(BF16)
                    pbias[c, h] = both[DK:] + shift

    for group, home in homes:
        for to_readers in (False, True):

            @pl.when(home & (pair > 0) & ((pair == last_pair - 1) if to_readers else (pair < last_pair - 1)))
            def _():
                for h in group:
                    for c in (0, 1):
                        pass_on(c, h, to_readers)
                    for c in (0, 1):
                        between(c, h)

    @pl.when((late == 1) & (pair == last_pair))
    def _():
        for h in range(heads):
            to_later(h).wait_recv()
        for h in range(heads):
            moved = dot_nt(reach[h], far_maps[core, h])
            moved = moved[:tok] + moved[tok:]
            reach[h, :tok], reach[h, tok:] = split2(moved[:, :DK])
            loc[h] += moved[:, DK:]

    @pl.when((pair == 0) & (late == 0))
    def _():
        sin[...] = jnp.zeros_like(sin)

    for group in (odds, evens):
        to_homes(group, lambda copy: copy.wait_send())

    @pl.when((pair == 0) & (late == 0))
    def _():
        for h in range(heads):
            first_state(h).wait_send()

    @pl.when((pair == last_pair) & (late == 0))
    def _():
        for h in range(heads):
            to_later(h).wait_send()

    loads[6].wait()
    loads[7].wait()

    def read(lo, hi):
        for h in range(lo, hi):
            at_home = middle & (late == 1 - h % 2) & (core == 1)

            @pl.when(jnp.logical_not(at_home | ((pair == 0) & (late == 0))))
            def _():
                first_state(h).wait_recv()

        for h in range(lo, hi):
            seen = dot_nt(reach[h], sin[h])
            att = loc[h] + (seen[:tok] + seen[tok:])
            inv = lax.rsqrt(jnp.mean(att * att, axis=-1, keepdims=True) + 1e-05)
            nrm[h] = (att * inv * gain_ref[:, h * DV : (h + 1) * DV]).astype(BF16)
        for h in range(lo, hi):
            cross(h).start()

    def mine(h):
        return nrm[h, pl.ds(pl.multiple_of(core * half, half), half), :]

    def theirs(lo, hi):
        for h in range(lo, hi):
            cross(h).wait_recv()
        return dot(jnp.concatenate([nrm_oth[h] for h in range(lo, hi)], axis=1), w_oth[lo * DV : hi * DV])

    cut = heads // 2
    read(0, cut)
    acc[...] = dot(jnp.concatenate([mine(h) for h in range(cut)], axis=1), w_own[: cut * DV])
    read(cut, heads)
    weights.wait_recv()
    acc[...] += theirs(0, cut)
    acc[...] += dot(jnp.concatenate([mine(h) for h in range(cut, heads)], axis=1), w_own[cut * DV :])
    out_ref[...] = (acc[...] + theirs(cut, heads)).astype(BF16)

    for h in range(heads):
        cross(h).wait_send()
    weights.wait_send()
    for group, home in homes:
        for to_readers in (False, True):

            @pl.when(home & ((pair == last_pair - 1) if to_readers else (pair < last_pair - 1)))
            def _():
                for h in group:
                    for c in range(2):
                        for copy in leave(c, h, to_readers):
                            copy.wait_send()

        @pl.when(home & (pair > 0))
        def _():
            for h in group:
                to_sibling(h).wait_send()
                for c in range(2):
                    to_partner(c, h).wait_send()


def shards(queries, key_rows, value_rows, strengths, log_gate, keep_flag, norm_gain, out_weight):
    tok = queries.shape[0]
    heads = strengths.shape[0]
    size = 2 * tok
    wide = out_weight.shape[1]
    hbm = pl.BlockSpec(memory_space=pltpu.HBM)
    vmem = pl.BlockSpec(memory_space=pltpu.VMEM)
    dma = pltpu.SemaphoreType.DMA
    operands = (
        queries, key_rows, value_rows, strengths, log_gate, keep_flag[None, :], norm_gain[None, :], out_weight,
    )
    return pl.pallas_call(
        functools.partial(pair_kernel, heads),
        out_shape=jax.ShapeDtypeStruct((tok // 2, wide), BF16),
        in_specs=[hbm] * len(operands),
        out_specs=vmem,
        scratch_shapes=[
            pltpu.VMEM(key_rows.shape, BF16),
            pltpu.VMEM(value_rows.shape, BF16),
            pltpu.VMEM((size, heads * DK), BF16),
            pltpu.VMEM(queries.shape, BF16),
            pltpu.VMEM(strengths.shape, F32),
            pltpu.VMEM(log_gate.shape, F32),
            pltpu.VMEM((1, tok), jnp.int32),
            pltpu.VMEM((1, heads * DV), F32),
            pltpu.VMEM(out_weight.shape, BF16),
            pltpu.VMEM(out_weight.shape, BF16),
            pltpu.VMEM((16, size), F32),
            pltpu.VMEM((heads, DK, size), BF16),
            pltpu.VMEM((heads, DV, size), BF16),
            pltpu.VMEM((heads, size, size), BF16),
            pltpu.VMEM((heads, size, size), BF16),
            pltpu.VMEM((heads, tok, size), F32),
            pltpu.VMEM((heads, tok, tok), F32),
            pltpu.VMEM((heads, size, size), BF16),
            pltpu.VMEM((heads, DK + DV, size), BF16),
            pltpu.VMEM((heads, DK + DV, size), BF16),
            pltpu.VMEM((heads, size, DK), BF16),
            pltpu.VMEM((heads, DK + DV, DK), BF16),
            pltpu.VMEM((heads, DV, DK), F32),
            pltpu.VMEM((heads, DK + DV, DK), BF16),
            pltpu.VMEM((2, heads, DK + DV, DK), BF16),
            pltpu.VMEM((2, heads, DK, DK), BF16),
            pltpu.VMEM((2, heads, DV, DK), F32),
            pltpu.VMEM((2, heads, DV, DK), BF16),
            pltpu.VMEM((heads, DV, DK), BF16),
            pltpu.VMEM((2, heads, DV, DK), BF16),
            pltpu.VMEM((2, heads, DV, DK), BF16),
            pltpu.VMEM((heads, 2 * tok, DK), BF16),
            pltpu.VMEM((heads, tok, DV), F32),
            pltpu.VMEM((heads, tok, DV), BF16),
            pltpu.VMEM((heads, tok // 2, DV), BF16),
            pltpu.VMEM((tok // 2, wide), F32),
            dma((len(operands),)),
            dma((heads,)),
            dma((heads,)),
            dma((2 * heads,)),
            dma((heads,)),
            dma((2 * heads,)),
            dma((4 * heads,)),
            dma((2 * heads,)),
            dma((heads,)),
            dma((heads,)),
            dma((heads,)),
            dma(()),
            dma(()),
        ],
        compiler_params=pltpu.CompilerParams(vmem_limit_bytes=28 << 20, collective_id=0, has_side_effects=True),
        name="pair_project",
    )(*(pltpu.with_memory_space_constraint(x, pltpu.HBM) for x in operands))


def solution(mesh):
    in_specs = (
        P(("groups", "seq"), "head"),
        P(("groups", "seq"), None, "head"),
        P(("groups", "seq"), None, "head"),
        P("head", None, ("groups", "seq")),
        P("head", ("groups", "seq")),
        P(("groups", "seq")),
        P("head"),
        P("head", None),
    )
    out_specs = P(("groups", "seq", "head"), None)
    return jax.shard_map(shards, mesh=mesh, in_specs=in_specs, out_specs=out_specs, check_vma=False)
```

```python
import functools

import jax
import jax.numpy as jnp
from jax import lax
from jax.experimental import pallas as pl
from jax.experimental.pallas import tpu as pltpu
from jax.sharding import PartitionSpec as P

DK = 128
DV = 128
F32 = jnp.float32
BF16 = jnp.bfloat16
MESH = pl.DeviceIdType.MESH


def split2(x):
    hi = x.astype(BF16)
    return hi, (x - hi.astype(F32)).astype(BF16)


def split3(x):
    a = x.astype(BF16)
    rest = x - a.astype(F32)
    b = rest.astype(BF16)
    return a, b, (rest - b.astype(F32)).astype(BF16)


def dot(a, b):
    return jnp.dot(a, b, preferred_element_type=F32)


def dot_nt(a, b):
    return lax.dot_general(a, b, (((1,), (1,)), ((), ())), preferred_element_type=F32)


def iotas(rows, cols):
    return lax.broadcasted_iota(jnp.int32, (rows, cols), 0), lax.broadcasted_iota(jnp.int32, (rows, cols), 1)


def pair_kernel(
    heads, q_hbm, k_hbm, v_hbm, str_hbm, log_hbm, keep_hbm, gain_hbm, w_hbm, out_ref,
    k_raw, v_raw, k_ref, q_ref, str_ref, log_ref, keep_ref, gain_ref, w_own, w_oth,
    small, kt, vt, a_hi, a_lo, c_top, c_low, xt, w0, res, xk, maps, bias, near_maps, far_maps, pmap, pbias, cin, sin, sout, smid,
    reach, loc, nrm, nrm_oth, acc,
    load_sem, map_send, near_recv, far_recv, mid_send, far_send, out_send, cin_recv, sin_recv,
    nrm_send, nrm_recv, w_send, w_recv,
):
    tok = q_ref.shape[0]
    size = 2 * tok
    n = lax.axis_size("seq")
    me = lax.axis_index("seq")
    core = lax.axis_index("head")
    sibling = 1 - core
    late = lax.rem(me, 2)
    pair = me // 2
    last_pair = n // 2 - 1
    partner = me + 1 - 2 * late
    near = lax.rem(me + 2, n)
    evens, odds = range(0, heads, 2), range(1, heads, 2)
    inside = pair < last_pair
    middle = inside & (pair > 0)
    homes = ((evens, inside & (late == 1) & (core == 1)), (odds, inside & (late == 0) & (core == 1)))

    pairs = (
        (str_hbm, str_ref),
        (log_hbm, log_ref),
        (keep_hbm, keep_ref),
        (k_hbm, k_raw),
        (v_hbm, v_raw),
        (q_hbm, q_ref),
        (gain_hbm, gain_ref),
        (w_hbm, w_own),
    )
    loads = [pltpu.make_async_copy(a, b, load_sem.at[i]) for i, (a, b) in enumerate(pairs)]
    for load in loads[:7]:
        load.start()

    barrier = pltpu.get_barrier_semaphore()

    def signal(where):
        pl.semaphore_signal(barrier, inc=1, device_id=where, device_id_type=MESH)

    signal({"head": sibling})
    for c in range(2):
        signal({"seq": partner, "head": c})

    @pl.when((pair < last_pair - 1) & (core == 1))
    def _():
        signal({"seq": near, "head": 1})

    @pl.when((pair == last_pair - 1) & (core == 1))
    def _():
        for c in range(2):
            signal({"seq": near, "head": c})
            signal({"seq": lax.rem(me + 3 - 2 * late, n), "head": c})

    @pl.when(middle & (core == 1))
    def _():
        signal({"seq": me - 2, "head": 1})

    @pl.when((pair == last_pair) & (pair > 0))
    def _():
        signal({"seq": me - 2, "head": 1})
        signal({"seq": me - 1 - 2 * late, "head": 1})

    peers = (
        3
        + jnp.where((pair < last_pair - 1) & (core == 1), 1, 0)
        + jnp.where((pair == last_pair - 1) & (core == 1), 4, 0)
        + jnp.where(middle & (core == 1), 1, 0)
        + jnp.where((pair == last_pair) & (pair > 0), 2, 0)
    )

    def remote(src, dst, ssem, rsem, where):
        return pltpu.make_async_remote_copy(
            src_ref=src, dst_ref=dst, send_sem=ssem, recv_sem=rsem, device_id=where, device_id_type=MESH
        )

    def flat(c, h):
        return c * heads + h

    every, bias_only = pl.ds(0, DK + DV), pl.ds(DK, DV)

    def over(h):
        return lambda span: remote(
            maps.at[h, span], near_maps.at[h, span], map_send.at[h], near_recv.at[h], {"head": 1}
        )

    def across(c, h):
        return lambda span: remote(
            maps.at[h, span], far_maps.at[c, h, span], map_send.at[h], far_recv.at[flat(c, h)],
            {"seq": partner, "head": 1},
        )

    def to_homes(group, act):
        home_late = 0 if group is odds else 1
        start = inside & (pair == 0) & (late == 0)
        later = inside & jnp.logical_not((pair == 0) & (late == 0))
        for case, span in ((start, bias_only), (later, every)):

            @pl.when(case & (late != home_late))
            def _():
                for h in group:
                    act(across(core, h)(span))

            @pl.when(case & (late == home_late) & (core == 0))
            def _():
                for h in group:
                    act(over(h)(span))

    def to_later(h):
        return remote(
            maps.at[h], far_maps.at[core, h], map_send.at[h], far_recv.at[flat(core, h)], {"seq": partner}
        )

    def first_state(h):
        return remote(maps.at[h, pl.ds(DK, DV)], sin.at[h], mid_send.at[h], sin_recv.at[h], {"seq": partner})

    def leave(c, h, to_readers):
        if not to_readers:
            return [enter(c, h)]
        return [
            remote(
                sout.at[c, h], sin.at[h], out_send.at[2 * flat(c, h) + k], sin_recv.at[h], {"seq": target, "head": c}
            )
            for k, target in enumerate((lax.rem(me + 3 - 2 * late, n), near))
        ]

    def enter(c, h):
        return remote(
            sout.at[c, h], cin.at[c, h], out_send.at[2 * flat(c, h)], cin_recv.at[flat(c, h)],
            {"seq": near, "head": 1},
        )

    def to_sibling(h):
        src = smid.at[0, h] if h % 2 == 0 else cin.at[0, h]
        return remote(src, sin.at[h], mid_send.at[h], sin_recv.at[h], {"head": 0})

    def to_partner(c, h):
        src = cin.at[c, h] if h % 2 == 0 else smid.at[c, h]
        return remote(src, sin.at[h], far_send.at[flat(c, h)], sin_recv.at[h], {"seq": partner, "head": c})

    half = tok // 2

    def cross(h):
        span = pl.ds(pl.multiple_of(sibling * half, half), half)
        return remote(nrm.at[h, span], nrm_oth.at[h], nrm_send.at[h], nrm_recv.at[h], {"head": sibling})

    weights = remote(w_hbm, w_oth, w_send, w_recv, {"head": sibling})

    for load in loads[:3]:
        load.wait()
    live = keep_ref[...].astype(F32)
    small[...] = jnp.zeros_like(small)
    small[:heads, :tok] = str_ref[:, 0, :] * live
    small[:heads, tok:] = str_ref[:, 1, :] * live
    small[8 : 8 + heads, :tok] = log_ref[...] * live
    r_i, c_i = iotas(size, size)
    place = jnp.where(jnp.where(r_i < tok, 2 * r_i, 2 * (r_i - tok) + 1) == c_i, 1.0, 0.0).astype(BF16)
    r_t, c_t = iotas(tok, size)
    upto = jnp.where(2 * r_t <= c_t, 1.0, 0.0).astype(BF16)
    r_c, c_c = iotas(size, tok)
    upto_c = jnp.where(2 * c_c <= r_c, 1.0, 0.0).astype(BF16)
    s3 = split3(small[...])
    beta_rows = dot(s3[0][:8], place) + (dot(s3[1][:8], place) + dot(s3[2][:8], place))
    logs = [s[8:, :tok] for s in s3]
    cum_rows = dot(logs[0], upto) + (dot(logs[1], upto) + dot(logs[2], upto))
    cum_cols = dot_nt(upto_c, logs[0]) + (dot_nt(upto_c, logs[1]) + dot_nt(upto_c, logs[2]))

    loads[3].wait()
    loads[7].start()
    k_ref[...] = k_raw[...].reshape(k_ref.shape)
    row_t, col_t = iotas(tok, tok)
    after = col_t > row_t
    after_top = c_t > r_t
    eye = jnp.where(row_t == col_t, 1.0, 0.0)
    betas, cums, squares = [], [], []
    for h in range(heads):
        span = slice(h * DK, (h + 1) * DK)
        kt[h] = k_ref[:, span].T
        ktf = kt[h].astype(F32)
        ss = jnp.sum(ktf * ktf, axis=0, keepdims=True) + 1e-06
        beta = beta_rows[h : h + 1]
        cum = cum_rows[h : h + 1]
        betas.append(beta)
        cums.append(cum)
        squares.append(ss)
        scale = beta / ss
        cum_col = cum_cols[:, h : h + 1]
        top = (scale * jnp.exp(jnp.minimum(cum - cum_col[:tok], 0.0))) * dot(k_ref[:tok, span], kt[h])
        low = (scale[:, tok:] * jnp.exp(jnp.minimum(cum[:, tok:] - cum_col[tok:], 0.0))) * dot(
            k_ref[tok:, span], kt[h, :, tok:]
        )
        top = jnp.where(after_top, top, 0.0)
        low = jnp.where(after, low, 0.0)
        c_top[h] = top
        c_low[h] = low
        a_hi[h, :tok], a_lo[h, :tok] = split2(top)
        a_hi[h, tok:, tok:], a_lo[h, tok:, tok:] = split2(low)
        zero = jnp.zeros((tok, tok), BF16)
        a_hi[h, tok:, :tok] = zero
        a_lo[h, tok:, :tok] = zero
        xt[h, tok:, :tok] = zero


    eye_b = eye.astype(BF16)
    steps = tok.bit_length() - 1
    for bit in range(steps):
        step = 1 << bit
        spans = [slice(0, tok)] if step < 16 else [slice(at, at + step) for at in range(0, tok, 2 * step)]

        def take(ref_rows):
            return jnp.concatenate([ref_rows(span) for span in spans], axis=0)

        low_bit = take(lambda span: row_t[span]) >> bit
        picked = ((take(lambda span: col_t[span]) >> bit) == (low_bit | 1)) & ((low_bit & 1) == 0)
        for h in range(heads):
            for c_ref, at in ((c_top, 0), (c_low, tok)):
                own = slice(at, at + tok)
                side = c_ref.shape[2]
                m = jnp.where(picked, take(lambda span: c_ref[h, span, :tok]), 0.0).astype(BF16)
                first = 0 if bit + 1 < steps else tok
                x = eye_b if bit == 0 else xt[h, own, own]
                if step < 16:
                    c_hi, c_lo = split2(c_ref[h])
                    if bit > 0:
                        c_hi = jnp.concatenate([c_hi, x], axis=1)
                        c_lo = jnp.concatenate([c_lo, jnp.zeros_like(x)], axis=1)
                    moved = dot(jnp.concatenate([m, m], axis=1), jnp.concatenate([c_hi, c_lo], axis=0))
                elif side > first:
                    moved = dot(m, jnp.concatenate([c_ref[h, :, first:].astype(BF16), x], axis=1))
                else:
                    moved = dot(m, x)
                if bit == 0:
                    xt[h, own, own] = x
                done = 0
                for span in spans:
                    count = span.stop - span.start
                    part = slice(done, done + count)
                    if side > first:
                        c_ref[h, span, first:] -= moved[part, : side - first]
                    gone = m[part] if bit == 0 else moved[part, side - first :].astype(BF16)
                    rows_at = slice(at + span.start, at + span.stop)
                    xt[h, rows_at, own] = x[span] - gone
                    done += count
    for h in range(heads):
        xt[h, :tok, tok:] = -dot(c_top[h, :, tok:].astype(BF16), xt[h, tok:, tok:]).astype(BF16)

    pl.semaphore_wait(barrier, peers)
    weights.start()
    loads[4].wait()
    v_flat = v_raw[...].reshape(k_ref.shape)
    for h in range(heads):
        vt[h] = v_flat[:, h * DV : (h + 1) * DV].T

    for group in (odds, evens):
        rhs, fade = {}, {}
        for h in group:
            beta, cum, ss = betas[h], cums[h], squares[h]
            rhs[h] = jnp.concatenate(
                [(beta * jnp.exp(cum) / ss) * kt[h].astype(F32), (beta * lax.rsqrt(ss)) * vt[h].astype(F32)], axis=0
            )
            fade[h] = jnp.exp(cum[:, size - 1 : size] - cum)
        for h in group:
            w0[h] = dot(rhs[h].astype(BF16), xt[h]).astype(BF16)
        for h in group:
            keys = k_ref[:, h * DK : (h + 1) * DK]
            xk[h] = dot((xt[h].astype(F32) * fade[h]).astype(BF16), keys).astype(BF16)
        for h in group:
            twice = jnp.concatenate([w0[h], w0[h]], axis=1)
            res[h] = (rhs[h] - w0[h].astype(F32) - dot(twice, jnp.concatenate([a_hi[h], a_lo[h]], axis=0))).astype(BF16)
        for h in group:
            keys = k_ref[:, h * DK : (h + 1) * DK]
            faded = split2(w0[h].astype(F32) * fade[h])
            tb = dot(
                jnp.concatenate([faded[0], faded[1], res[h]], axis=1), jnp.concatenate([keys, keys, xk[h]], axis=0)
            )
            maps[h, :DK] = (eye * jnp.exp(cums[h][:, size - 1 : size]) - tb[:DK]).astype(BF16)
            maps[h, DK:] = tb[DK:].astype(BF16)
            bias[h] = tb[DK:]

        to_homes(group, lambda copy: copy.start())

    @pl.when((pair == 0) & (late == 0))
    def _():
        for h in range(heads):
            first_state(h).start()

    @pl.when((pair == last_pair) & (late == 0))
    def _():
        for h in range(heads):
            to_later(h).start()

    loads[5].wait()
    t_i, l_i = iotas(tok, size)
    visible = l_i <= 2 * t_i + 1
    tok_r, tok_c = iotas(tok, tok)
    upto_t = jnp.where(tok_c <= tok_r, 1.0, 0.0).astype(BF16)
    cum_toks = dot_nt(upto_t, logs[0]) + (dot_nt(upto_t, logs[1]) + dot_nt(upto_t, logs[2]))
    for h in range(heads):
        q = q_ref[:, h * DK : (h + 1) * DK]
        qf = q.astype(F32)
        rq = lax.rsqrt(jnp.sum(qf * qf, axis=-1, keepdims=True) + 1e-06)
        cum_tok = cum_toks[:, h : h + 1]
        decay = jnp.where(visible, jnp.exp(jnp.minimum(cum_tok - cums[h], 0.0)), 0.0)
        mix = split2((rq * decay) * dot(q, kt[h]))
        w = split2(w0[h].astype(F32) + dot(res[h], xt[h]))
        both = dot_nt(mix[0], w[0]) + (dot_nt(mix[0], w[1]) + dot_nt(mix[1], w[0]))
        reach[h, :tok], reach[h, tok:] = split2((jnp.exp(cum_tok) * rq) * qf - both[:, :DK])
        loc[h] = both[:, DK:]

    def arrive(c, h, first):
        own_map = maps.at[h] if c == 1 else near_maps.at[h]
        if c == 0:
            over(h)(bias_only if first and h % 2 == 1 else every).wait_recv()
        across(c, h)(bias_only if first and h % 2 == 0 else every).wait_recv()
        one, two = (far_maps.at[c, h], own_map) if h % 2 == 0 else (own_map, far_maps.at[c, h])
        exact = c == 1 and h % 2 == 0
        return one, two[:DK], bias[h] if exact else two[DK:].astype(F32)

    def pass_on(c, h, to_readers):
        enter(c, h).wait_recv()
        sout[c, h] = (dot(cin[c, h], pmap[c, h]) + pbias[c, h]).astype(BF16)
        for copy in leave(c, h, to_readers):
            copy.start()
        if h % 2 == 0:
            to_partner(c, h).start()
        elif c == 0:
            to_sibling(h).start()
        else:
            sin[h] = cin[c, h]

    def between(c, h):
        if h % 2 == 0:
            one, shift = far_maps.at[c, h], far_maps[c, h, DK:].astype(F32)
        elif c == 1:
            one, shift = maps.at[h], bias[h]
        else:
            one, shift = near_maps.at[h], near_maps[h, DK:].astype(F32)
        smid[c, h] = (dot(cin[c, h], one[:DK]) + shift).astype(BF16)
        if h % 2 == 1:
            to_partner(c, h).start()
        elif c == 0:
            to_sibling(h).start()
        else:
            sin[h] = smid[c, h]

    for group, home in homes:

        @pl.when(home & (pair == 0))
        def _():
            for h in group:
                for c in (1, 0):
                    one, trans, shift = arrive(c, h, True)
                    sout[c, h] = (dot(one[DK:], trans) + shift).astype(BF16)
                    for copy in leave(c, h, last_pair == 1):
                        copy.start()

        @pl.when(home & (pair > 0))
        def _():
            for h in group:
                for c in (1, 0):
                    one, trans, shift = arrive(c, h, False)
                    both = dot(one[...], trans)
                    pmap[c, h] = both[:DK].astype(BF16)
                    pbias[c, h] = both[DK:] + shift

    for group, home in homes:
        for to_readers in (False, True):

            @pl.when(home & (pair > 0) & ((pair == last_pair - 1) if to_readers else (pair < last_pair - 1)))
            def _():
                for c in (0, 1):
                    for h in group:
                        pass_on(c, h, to_readers)
                    for h in group:
                        between(c, h)

    @pl.when((late == 1) & (pair == last_pair))
    def _():
        for h in range(heads):
            to_later(h).wait_recv()
        for h in range(heads):
            moved = dot_nt(reach[h], far_maps[core, h])
            moved = moved[:tok] + moved[tok:]
            reach[h, :tok], reach[h, tok:] = split2(moved[:, :DK])
            loc[h] += moved[:, DK:]

    @pl.when((pair == 0) & (late == 0))
    def _():
        sin[...] = jnp.zeros_like(sin)

    for group in (odds, evens):
        to_homes(group, lambda copy: copy.wait_send())

    @pl.when((pair == 0) & (late == 0))
    def _():
        for h in range(heads):
            first_state(h).wait_send()

    @pl.when((pair == last_pair) & (late == 0))
    def _():
        for h in range(heads):
            to_later(h).wait_send()

    loads[6].wait()
    loads[7].wait()

    def read(lo, hi):
        for h in range(lo, hi):
            at_home = middle & (late == 1 - h % 2) & (core == 1)

            @pl.when(jnp.logical_not(at_home | ((pair == 0) & (late == 0))))
            def _():
                first_state(h).wait_recv()

        for h in range(lo, hi):
            seen = dot_nt(reach[h], sin[h])
            att = loc[h] + (seen[:tok] + seen[tok:])
            inv = lax.rsqrt(jnp.mean(att * att, axis=-1, keepdims=True) + 1e-05)
            nrm[h] = (att * inv * gain_ref[:, h * DV : (h + 1) * DV]).astype(BF16)
        for h in range(lo, hi):
            cross(h).start()

    def mine(h):
        return nrm[h, pl.ds(pl.multiple_of(core * half, half), half), :]

    def theirs(lo, hi):
        for h in range(lo, hi):
            cross(h).wait_recv()
        return dot(jnp.concatenate([nrm_oth[h] for h in range(lo, hi)], axis=1), w_oth[lo * DV : hi * DV])

    cut = heads // 2
    read(0, cut)
    acc[...] = dot(jnp.concatenate([mine(h) for h in range(cut)], axis=1), w_own[: cut * DV])
    read(cut, heads)
    weights.wait_recv()
    acc[...] += theirs(0, cut)
    acc[...] += dot(jnp.concatenate([mine(h) for h in range(cut, heads)], axis=1), w_own[cut * DV :])
    out_ref[...] = (acc[...] + theirs(cut, heads)).astype(BF16)

    for h in range(heads):
        cross(h).wait_send()
    weights.wait_send()
    for group, home in homes:
        for to_readers in (False, True):

            @pl.when(home & ((pair == last_pair - 1) if to_readers else (pair < last_pair - 1)))
            def _():
                for h in group:
                    for c in range(2):
                        for copy in leave(c, h, to_readers):
                            copy.wait_send()

        @pl.when(home & (pair > 0))
        def _():
            for h in group:
                to_sibling(h).wait_send()
                for c in range(2):
                    to_partner(c, h).wait_send()


def shards(queries, key_rows, value_rows, strengths, log_gate, keep_flag, norm_gain, out_weight):
    tok = queries.shape[0]
    heads = strengths.shape[0]
    size = 2 * tok
    wide = out_weight.shape[1]
    hbm = pl.BlockSpec(memory_space=pltpu.HBM)
    vmem = pl.BlockSpec(memory_space=pltpu.VMEM)
    dma = pltpu.SemaphoreType.DMA
    operands = (
        queries, key_rows, value_rows, strengths, log_gate, keep_flag[None, :], norm_gain[None, :], out_weight,
    )
    return pl.pallas_call(
        functools.partial(pair_kernel, heads),
        out_shape=jax.ShapeDtypeStruct((tok // 2, wide), BF16),
        in_specs=[hbm] * len(operands),
        out_specs=vmem,
        scratch_shapes=[
            pltpu.VMEM(key_rows.shape, BF16),
            pltpu.VMEM(value_rows.shape, BF16),
            pltpu.VMEM((size, heads * DK), BF16),
            pltpu.VMEM(queries.shape, BF16),
            pltpu.VMEM(strengths.shape, F32),
            pltpu.VMEM(log_gate.shape, F32),
            pltpu.VMEM((1, tok), jnp.int32),
            pltpu.VMEM((1, heads * DV), F32),
            pltpu.VMEM(out_weight.shape, BF16),
            pltpu.VMEM(out_weight.shape, BF16),
            pltpu.VMEM((16, size), F32),
            pltpu.VMEM((heads, DK, size), BF16),
            pltpu.VMEM((heads, DV, size), BF16),
            pltpu.VMEM((heads, size, size), BF16),
            pltpu.VMEM((heads, size, size), BF16),
            pltpu.VMEM((heads, tok, size), F32),
            pltpu.VMEM((heads, tok, tok), F32),
            pltpu.VMEM((heads, size, size), BF16),
            pltpu.VMEM((heads, DK + DV, size), BF16),
            pltpu.VMEM((heads, DK + DV, size), BF16),
            pltpu.VMEM((heads, size, DK), BF16),
            pltpu.VMEM((heads, DK + DV, DK), BF16),
            pltpu.VMEM((heads, DV, DK), F32),
            pltpu.VMEM((heads, DK + DV, DK), BF16),
            pltpu.VMEM((2, heads, DK + DV, DK), BF16),
            pltpu.VMEM((2, heads, DK, DK), BF16),
            pltpu.VMEM((2, heads, DV, DK), F32),
            pltpu.VMEM((2, heads, DV, DK), BF16),
            pltpu.VMEM((heads, DV, DK), BF16),
            pltpu.VMEM((2, heads, DV, DK), BF16),
            pltpu.VMEM((2, heads, DV, DK), BF16),
            pltpu.VMEM((heads, 2 * tok, DK), BF16),
            pltpu.VMEM((heads, tok, DV), F32),
            pltpu.VMEM((heads, tok, DV), BF16),
            pltpu.VMEM((heads, tok // 2, DV), BF16),
            pltpu.VMEM((tok // 2, wide), F32),
            dma((len(operands),)),
            dma((heads,)),
            dma((heads,)),
            dma((2 * heads,)),
            dma((heads,)),
            dma((2 * heads,)),
            dma((4 * heads,)),
            dma((2 * heads,)),
            dma((heads,)),
            dma((heads,)),
            dma((heads,)),
            dma(()),
            dma(()),
        ],
        compiler_params=pltpu.CompilerParams(vmem_limit_bytes=28 << 20, collective_id=0, has_side_effects=True),
        name="pair_project",
    )(*(pltpu.with_memory_space_constraint(x, pltpu.HBM) for x in operands))


def solution(mesh):
    in_specs = (
        P(("groups", "seq"), "head"),
        P(("groups", "seq"), None, "head"),
        P(("groups", "seq"), None, "head"),
        P("head", None, ("groups", "seq")),
        P("head", ("groups", "seq")),
        P(("groups", "seq")),
        P("head"),
        P("head", None),
    )
    out_specs = P(("groups", "seq", "head"), None)
    return jax.shard_map(shards, mesh=mesh, in_specs=in_specs, out_specs=out_specs, check_vma=False)
```

```python
import functools

import jax
import jax.numpy as jnp
from jax import lax
from jax.experimental import pallas as pl
from jax.experimental.pallas import tpu as pltpu
from jax.sharding import PartitionSpec as P

DK = 128
DV = 128
F32 = jnp.float32
BF16 = jnp.bfloat16
MESH = pl.DeviceIdType.MESH


def split2(x):
    hi = x.astype(BF16)
    return hi, (x - hi.astype(F32)).astype(BF16)


def split3(x):
    a = x.astype(BF16)
    rest = x - a.astype(F32)
    b = rest.astype(BF16)
    return a, b, (rest - b.astype(F32)).astype(BF16)


def dot(a, b):
    return jnp.dot(a, b, preferred_element_type=F32)


def dot_nt(a, b):
    return lax.dot_general(a, b, (((1,), (1,)), ((), ())), preferred_element_type=F32)


def iotas(rows, cols):
    return lax.broadcasted_iota(jnp.int32, (rows, cols), 0), lax.broadcasted_iota(jnp.int32, (rows, cols), 1)


def pair_kernel(
    heads, q_hbm, k_hbm, v_hbm, str_hbm, log_hbm, keep_hbm, gain_hbm, w_hbm, out_ref,
    k_raw, v_raw, k_ref, q_ref, str_ref, log_ref, keep_ref, gain_ref, w_own, w_oth,
    small, kt, vt, a_hi, a_lo, c_top, c_low, xt, w0, res, xk, maps, bias, near_maps, far_maps, pmap, pbias, cin, sin, sout, smid,
    reach, loc, nrm, nrm_oth, acc,
    load_sem, map_send, near_recv, far_recv, mid_send, far_send, out_send, cin_recv, sin_recv,
    nrm_send, nrm_recv, w_send, w_recv,
):
    tok = q_ref.shape[0]
    size = 2 * tok
    n = lax.axis_size("seq")
    me = lax.axis_index("seq")
    core = lax.axis_index("head")
    sibling = 1 - core
    late = lax.rem(me, 2)
    pair = me // 2
    last_pair = n // 2 - 1
    partner = me + 1 - 2 * late
    near = lax.rem(me + 2, n)
    evens, odds = range(0, heads, 2), range(1, heads, 2)
    inside = pair < last_pair
    middle = inside & (pair > 0)
    homes = ((evens, inside & (late == 1) & (core == 1)), (odds, inside & (late == 0) & (core == 1)))

    pairs = (
        (str_hbm, str_ref),
        (log_hbm, log_ref),
        (keep_hbm, keep_ref),
        (k_hbm, k_raw),
        (v_hbm, v_raw),
        (q_hbm, q_ref),
        (gain_hbm, gain_ref),
        (w_hbm, w_own),
    )
    loads = [pltpu.make_async_copy(a, b, load_sem.at[i]) for i, (a, b) in enumerate(pairs)]
    for load in loads[:4]:
        load.start()

    barrier = pltpu.get_barrier_semaphore()

    def signal(where):
        pl.semaphore_signal(barrier, inc=1, device_id=where, device_id_type=MESH)

    signal({"head": sibling})
    for c in range(2):
        signal({"seq": partner, "head": c})

    @pl.when((pair < last_pair - 1) & (core == 1))
    def _():
        signal({"seq": near, "head": 1})

    @pl.when((pair == last_pair - 1) & (core == 1))
    def _():
        for c in range(2):
            signal({"seq": near, "head": c})
            signal({"seq": lax.rem(me + 3 - 2 * late, n), "head": c})

    @pl.when(middle & (core == 1))
    def _():
        signal({"seq": me - 2, "head": 1})

    @pl.when((pair == last_pair) & (pair > 0))
    def _():
        signal({"seq": me - 2, "head": 1})
        signal({"seq": me - 1 - 2 * late, "head": 1})

    peers = (
        3
        + jnp.where((pair < last_pair - 1) & (core == 1), 1, 0)
        + jnp.where((pair == last_pair - 1) & (core == 1), 4, 0)
        + jnp.where(middle & (core == 1), 1, 0)
        + jnp.where((pair == last_pair) & (pair > 0), 2, 0)
    )

    def remote(src, dst, ssem, rsem, where):
        return pltpu.make_async_remote_copy(
            src_ref=src, dst_ref=dst, send_sem=ssem, recv_sem=rsem, device_id=where, device_id_type=MESH
        )

    def flat(c, h):
        return c * heads + h

    every, bias_only = pl.ds(0, DK + DV), pl.ds(DK, DV)

    def over(h):
        return lambda span: remote(
            maps.at[h, span], near_maps.at[h, span], map_send.at[h], near_recv.at[h], {"head": 1}
        )

    def across(c, h):
        return lambda span: remote(
            maps.at[h, span], far_maps.at[c, h, span], map_send.at[h], far_recv.at[flat(c, h)],
            {"seq": partner, "head": 1},
        )

    def to_homes(group, act):
        home_late = 0 if group is odds else 1
        start = inside & (pair == 0) & (late == 0)
        later = inside & jnp.logical_not((pair == 0) & (late == 0))
        for case, span in ((start, bias_only), (later, every)):

            @pl.when(case & (late != home_late))
            def _():
                for h in group:
                    act(across(core, h)(span))

            @pl.when(case & (late == home_late) & (core == 0))
            def _():
                for h in group:
                    act(over(h)(span))

    def to_later(h):
        return remote(
            maps.at[h], far_maps.at[core, h], map_send.at[h], far_recv.at[flat(core, h)], {"seq": partner}
        )

    def first_state(h):
        return remote(maps.at[h, pl.ds(DK, DV)], sin.at[h], mid_send.at[h], sin_recv.at[h], {"seq": partner})

    def leave(c, h, to_readers):
        if not to_readers:
            return [enter(c, h)]
        return [
            remote(
                sout.at[c, h], sin.at[h], out_send.at[2 * flat(c, h) + k], sin_recv.at[h], {"seq": target, "head": c}
            )
            for k, target in enumerate((lax.rem(me + 3 - 2 * late, n), near))
        ]

    def enter(c, h):
        return remote(
            sout.at[c, h], cin.at[c, h], out_send.at[2 * flat(c, h)], cin_recv.at[flat(c, h)],
            {"seq": near, "head": 1},
        )

    def to_sibling(h):
        src = smid.at[0, h] if h % 2 == 0 else cin.at[0, h]
        return remote(src, sin.at[h], mid_send.at[h], sin_recv.at[h], {"head": 0})

    def to_partner(c, h):
        src = cin.at[c, h] if h % 2 == 0 else smid.at[c, h]
        return remote(src, sin.at[h], far_send.at[flat(c, h)], sin_recv.at[h], {"seq": partner, "head": c})

    half = tok // 2

    def cross(h):
        span = pl.ds(pl.multiple_of(sibling * half, half), half)
        return remote(nrm.at[h, span], nrm_oth.at[h], nrm_send.at[h], nrm_recv.at[h], {"head": sibling})

    weights = remote(w_hbm, w_oth, w_send, w_recv, {"head": sibling})

    for load in loads[:3]:
        load.wait()
    live = keep_ref[...].astype(F32)
    small[...] = jnp.zeros_like(small)
    small[:heads, :tok] = str_ref[:, 0, :] * live
    small[:heads, tok:] = str_ref[:, 1, :] * live
    small[8 : 8 + heads, :tok] = log_ref[...] * live
    r_i, c_i = iotas(size, size)
    place = jnp.where(jnp.where(r_i < tok, 2 * r_i, 2 * (r_i - tok) + 1) == c_i, 1.0, 0.0).astype(BF16)
    r_t, c_t = iotas(tok, size)
    upto = jnp.where(2 * r_t <= c_t, 1.0, 0.0).astype(BF16)
    r_c, c_c = iotas(size, tok)
    upto_c = jnp.where(2 * c_c <= r_c, 1.0, 0.0).astype(BF16)
    s3 = split3(small[...])
    beta_rows = dot(s3[0][:8], place) + (dot(s3[1][:8], place) + dot(s3[2][:8], place))
    logs = [s[8:, :tok] for s in s3]
    cum_rows = dot(logs[0], upto) + (dot(logs[1], upto) + dot(logs[2], upto))
    cum_cols = dot_nt(upto_c, logs[0]) + (dot_nt(upto_c, logs[1]) + dot_nt(upto_c, logs[2]))

    loads[3].wait()
    for load in loads[4:]:
        load.start()
    k_ref[...] = k_raw[...].reshape(k_ref.shape)
    row_t, col_t = iotas(tok, tok)
    after = col_t > row_t
    after_top = c_t > r_t
    eye = jnp.where(row_t == col_t, 1.0, 0.0)
    betas, cums, squares = [], [], []
    for h in range(heads):
        span = slice(h * DK, (h + 1) * DK)
        kt[h] = k_ref[:, span].T
        ktf = kt[h].astype(F32)
        ss = jnp.sum(ktf * ktf, axis=0, keepdims=True) + 1e-06
        beta = beta_rows[h : h + 1]
        cum = cum_rows[h : h + 1]
        betas.append(beta)
        cums.append(cum)
        squares.append(ss)
        scale = beta / ss
        cum_col = cum_cols[:, h : h + 1]
        top = (scale * jnp.exp(jnp.minimum(cum - cum_col[:tok], 0.0))) * dot(k_ref[:tok, span], kt[h])
        low = (scale[:, tok:] * jnp.exp(jnp.minimum(cum[:, tok:] - cum_col[tok:], 0.0))) * dot(
            k_ref[tok:, span], kt[h, :, tok:]
        )
        top = jnp.where(after_top, top, 0.0)
        low = jnp.where(after, low, 0.0)
        c_top[h] = top
        c_low[h] = low
        a_hi[h, :tok], a_lo[h, :tok] = split2(top)
        a_hi[h, tok:, tok:], a_lo[h, tok:, tok:] = split2(low)
        zero = jnp.zeros((tok, tok), BF16)
        a_hi[h, tok:, :tok] = zero
        a_lo[h, tok:, :tok] = zero
        xt[h, tok:, :tok] = zero


    eye_b = eye.astype(BF16)
    steps = tok.bit_length() - 1
    for bit in range(steps):
        step = 1 << bit
        spans = [slice(0, tok)] if step < 16 else [slice(at, at + step) for at in range(0, tok, 2 * step)]

        def take(ref_rows):
            return jnp.concatenate([ref_rows(span) for span in spans], axis=0)

        low_bit = take(lambda span: row_t[span]) >> bit
        picked = ((take(lambda span: col_t[span]) >> bit) == (low_bit | 1)) & ((low_bit & 1) == 0)
        for h in range(heads):
            for c_ref, at in ((c_top, 0), (c_low, tok)):
                own = slice(at, at + tok)
                side = c_ref.shape[2]
                m = jnp.where(picked, take(lambda span: c_ref[h, span, :tok]), 0.0).astype(BF16)
                first = 0 if bit + 1 < steps else tok
                x = eye_b if bit == 0 else xt[h, own, own]
                if step < 16:
                    c_hi, c_lo = split2(c_ref[h])
                    if bit > 0:
                        c_hi = jnp.concatenate([c_hi, x], axis=1)
                        c_lo = jnp.concatenate([c_lo, jnp.zeros_like(x)], axis=1)
                    moved = dot(jnp.concatenate([m, m], axis=1), jnp.concatenate([c_hi, c_lo], axis=0))
                elif side > first:
                    moved = dot(m, jnp.concatenate([c_ref[h, :, first:].astype(BF16), x], axis=1))
                else:
                    moved = dot(m, x)
                if bit == 0:
                    xt[h, own, own] = x
                done = 0
                for span in spans:
                    count = span.stop - span.start
                    part = slice(done, done + count)
                    if side > first:
                        c_ref[h, span, first:] -= moved[part, : side - first]
                    gone = m[part] if bit == 0 else moved[part, side - first :].astype(BF16)
                    rows_at = slice(at + span.start, at + span.stop)
                    xt[h, rows_at, own] = x[span] - gone
                    done += count
    for h in range(heads):
        xt[h, :tok, tok:] = -dot(c_top[h, :, tok:].astype(BF16), xt[h, tok:, tok:]).astype(BF16)

    pl.semaphore_wait(barrier, peers)
    weights.start()
    loads[4].wait()
    v_flat = v_raw[...].reshape(k_ref.shape)
    for h in range(heads):
        vt[h] = v_flat[:, h * DV : (h + 1) * DV].T

    for group in (odds, evens):
        rhs, fade = {}, {}
        for h in group:
            beta, cum, ss = betas[h], cums[h], squares[h]
            rhs[h] = jnp.concatenate(
                [(beta * jnp.exp(cum) / ss) * kt[h].astype(F32), (beta * lax.rsqrt(ss)) * vt[h].astype(F32)], axis=0
            )
            fade[h] = jnp.exp(cum[:, size - 1 : size] - cum)
        for h in group:
            w0[h] = dot(rhs[h].astype(BF16), xt[h]).astype(BF16)
        for h in group:
            keys = k_ref[:, h * DK : (h + 1) * DK]
            xk[h] = dot((xt[h].astype(F32) * fade[h]).astype(BF16), keys).astype(BF16)
        for h in group:
            twice = jnp.concatenate([w0[h], w0[h]], axis=1)
            res[h] = (rhs[h] - w0[h].astype(F32) - dot(twice, jnp.concatenate([a_hi[h], a_lo[h]], axis=0))).astype(BF16)
        for h in group:
            keys = k_ref[:, h * DK : (h + 1) * DK]
            faded = split2(w0[h].astype(F32) * fade[h])
            tb = dot(
                jnp.concatenate([faded[0], faded[1], res[h]], axis=1), jnp.concatenate([keys, keys, xk[h]], axis=0)
            )
            maps[h, :DK] = (eye * jnp.exp(cums[h][:, size - 1 : size]) - tb[:DK]).astype(BF16)
            maps[h, DK:] = tb[DK:].astype(BF16)
            bias[h] = tb[DK:]

        to_homes(group, lambda copy: copy.start())

    @pl.when((pair == 0) & (late == 0))
    def _():
        for h in range(heads):
            first_state(h).start()

    @pl.when((pair == last_pair) & (late == 0))
    def _():
        for h in range(heads):
            to_later(h).start()

    loads[5].wait()
    t_i, l_i = iotas(tok, size)
    visible = l_i <= 2 * t_i + 1
    tok_r, tok_c = iotas(tok, tok)
    upto_t = jnp.where(tok_c <= tok_r, 1.0, 0.0).astype(BF16)
    cum_toks = dot_nt(upto_t, logs[0]) + (dot_nt(upto_t, logs[1]) + dot_nt(upto_t, logs[2]))
    for h in range(heads):
        q = q_ref[:, h * DK : (h + 1) * DK]
        qf = q.astype(F32)
        rq = lax.rsqrt(jnp.sum(qf * qf, axis=-1, keepdims=True) + 1e-06)
        cum_tok = cum_toks[:, h : h + 1]
        decay = jnp.where(visible, jnp.exp(jnp.minimum(cum_tok - cums[h], 0.0)), 0.0)
        mix = split2((rq * decay) * dot(q, kt[h]))
        w = split2(w0[h].astype(F32) + dot(res[h], xt[h]))
        both = dot_nt(mix[0], w[0]) + (dot_nt(mix[0], w[1]) + dot_nt(mix[1], w[0]))
        reach[h, :tok], reach[h, tok:] = split2((jnp.exp(cum_tok) * rq) * qf - both[:, :DK])
        loc[h] = both[:, DK:]

    def arrive(c, h, first):
        own_map = maps.at[h] if c == 1 else near_maps.at[h]
        if c == 0:
            over(h)(bias_only if first and h % 2 == 1 else every).wait_recv()
        across(c, h)(bias_only if first and h % 2 == 0 else every).wait_recv()
        one, two = (far_maps.at[c, h], own_map) if h % 2 == 0 else (own_map, far_maps.at[c, h])
        exact = c == 1 and h % 2 == 0
        return one, two[:DK], bias[h] if exact else two[DK:].astype(F32)

    def pass_on(c, h, to_readers):
        enter(c, h).wait_recv()
        sout[c, h] = (dot(cin[c, h], pmap[c, h]) + pbias[c, h]).astype(BF16)
        for copy in leave(c, h, to_readers):
            copy.start()
        if h % 2 == 0:
            to_partner(c, h).start()
        elif c == 0:
            to_sibling(h).start()
        else:
            sin[h] = cin[c, h]

    def between(c, h):
        if h % 2 == 0:
            one, shift = far_maps.at[c, h], far_maps[c, h, DK:].astype(F32)
        elif c == 1:
            one, shift = maps.at[h], bias[h]
        else:
            one, shift = near_maps.at[h], near_maps[h, DK:].astype(F32)
        smid[c, h] = (dot(cin[c, h], one[:DK]) + shift).astype(BF16)
        if h % 2 == 1:
            to_partner(c, h).start()
        elif c == 0:
            to_sibling(h).start()
        else:
            sin[h] = smid[c, h]

    for group, home in homes:

        @pl.when(home & (pair == 0))
        def _():
            for h in group:
                for c in (1, 0):
                    one, trans, shift = arrive(c, h, True)
                    sout[c, h] = (dot(one[DK:], trans) + shift).astype(BF16)
                    for copy in leave(c, h, last_pair == 1):
                        copy.start()

        @pl.when(home & (pair > 0))
        def _():
            for h in group:
                for c in (1, 0):
                    one, trans, shift = arrive(c, h, False)
                    both = dot(one[...], trans)
                    pmap[c, h] = both[:DK].astype(BF16)
                    pbias[c, h] = both[DK:] + shift

    for group, home in homes:
        for to_readers in (False, True):

            @pl.when(home & (pair > 0) & ((pair == last_pair - 1) if to_readers else (pair < last_pair - 1)))
            def _():
                for c in (0, 1):
                    for h in group:
                        pass_on(c, h, to_readers)
                for c in (0, 1):
                    for h in group:
                        between(c, h)

    @pl.when((late == 1) & (pair == last_pair))
    def _():
        for h in range(heads):
            to_later(h).wait_recv()
        for h in range(heads):
            moved = dot_nt(reach[h], far_maps[core, h])
            moved = moved[:tok] + moved[tok:]
            reach[h, :tok], reach[h, tok:] = split2(moved[:, :DK])
            loc[h] += moved[:, DK:]

    @pl.when((pair == 0) & (late == 0))
    def _():
        sin[...] = jnp.zeros_like(sin)

    for group in (odds, evens):
        to_homes(group, lambda copy: copy.wait_send())

    @pl.when((pair == 0) & (late == 0))
    def _():
        for h in range(heads):
            first_state(h).wait_send()

    @pl.when((pair == last_pair) & (late == 0))
    def _():
        for h in range(heads):
            to_later(h).wait_send()

    loads[6].wait()
    loads[7].wait()

    def read(lo, hi):
        for h in range(lo, hi):
            at_home = middle & (late == 1 - h % 2) & (core == 1)

            @pl.when(jnp.logical_not(at_home | ((pair == 0) & (late == 0))))
            def _():
                first_state(h).wait_recv()

        for h in range(lo, hi):
            seen = dot_nt(reach[h], sin[h])
            att = loc[h] + (seen[:tok] + seen[tok:])
            inv = lax.rsqrt(jnp.mean(att * att, axis=-1, keepdims=True) + 1e-05)
            nrm[h] = (att * inv * gain_ref[:, h * DV : (h + 1) * DV]).astype(BF16)
        for h in range(lo, hi):
            cross(h).start()

    def mine(h):
        return nrm[h, pl.ds(pl.multiple_of(core * half, half), half), :]

    def theirs(lo, hi):
        for h in range(lo, hi):
            cross(h).wait_recv()
        return dot(jnp.concatenate([nrm_oth[h] for h in range(lo, hi)], axis=1), w_oth[lo * DV : hi * DV])

    cut = heads // 2
    read(0, cut)
    acc[...] = dot(jnp.concatenate([mine(h) for h in range(cut)], axis=1), w_own[: cut * DV])
    read(cut, heads)
    weights.wait_recv()
    acc[...] += theirs(0, cut)
    acc[...] += dot(jnp.concatenate([mine(h) for h in range(cut, heads)], axis=1), w_own[cut * DV :])
    out_ref[...] = (acc[...] + theirs(cut, heads)).astype(BF16)

    for h in range(heads):
        cross(h).wait_send()
    weights.wait_send()
    for group, home in homes:
        for to_readers in (False, True):

            @pl.when(home & ((pair == last_pair - 1) if to_readers else (pair < last_pair - 1)))
            def _():
                for h in group:
                    for c in range(2):
                        for copy in leave(c, h, to_readers):
                            copy.wait_send()

        @pl.when(home & (pair > 0))
        def _():
            for h in group:
                to_sibling(h).wait_send()
                for c in range(2):
                    to_partner(c, h).wait_send()


def shards(queries, key_rows, value_rows, strengths, log_gate, keep_flag, norm_gain, out_weight):
    tok = queries.shape[0]
    heads = strengths.shape[0]
    size = 2 * tok
    wide = out_weight.shape[1]
    hbm = pl.BlockSpec(memory_space=pltpu.HBM)
    vmem = pl.BlockSpec(memory_space=pltpu.VMEM)
    dma = pltpu.SemaphoreType.DMA
    operands = (
        queries, key_rows, value_rows, strengths, log_gate, keep_flag[None, :], norm_gain[None, :], out_weight,
    )
    return pl.pallas_call(
        functools.partial(pair_kernel, heads),
        out_shape=jax.ShapeDtypeStruct((tok // 2, wide), BF16),
        in_specs=[hbm] * len(operands),
        out_specs=vmem,
        scratch_shapes=[
            pltpu.VMEM(key_rows.shape, BF16),
            pltpu.VMEM(value_rows.shape, BF16),
            pltpu.VMEM((size, heads * DK), BF16),
            pltpu.VMEM(queries.shape, BF16),
            pltpu.VMEM(strengths.shape, F32),
            pltpu.VMEM(log_gate.shape, F32),
            pltpu.VMEM((1, tok), jnp.int32),
            pltpu.VMEM((1, heads * DV), F32),
            pltpu.VMEM(out_weight.shape, BF16),
            pltpu.VMEM(out_weight.shape, BF16),
            pltpu.VMEM((16, size), F32),
            pltpu.VMEM((heads, DK, size), BF16),
            pltpu.VMEM((heads, DV, size), BF16),
            pltpu.VMEM((heads, size, size), BF16),
            pltpu.VMEM((heads, size, size), BF16),
            pltpu.VMEM((heads, tok, size), F32),
            pltpu.VMEM((heads, tok, tok), F32),
            pltpu.VMEM((heads, size, size), BF16),
            pltpu.VMEM((heads, DK + DV, size), BF16),
            pltpu.VMEM((heads, DK + DV, size), BF16),
            pltpu.VMEM((heads, size, DK), BF16),
            pltpu.VMEM((heads, DK + DV, DK), BF16),
            pltpu.VMEM((heads, DV, DK), F32),
            pltpu.VMEM((heads, DK + DV, DK), BF16),
            pltpu.VMEM((2, heads, DK + DV, DK), BF16),
            pltpu.VMEM((2, heads, DK, DK), BF16),
            pltpu.VMEM((2, heads, DV, DK), F32),
            pltpu.VMEM((2, heads, DV, DK), BF16),
            pltpu.VMEM((heads, DV, DK), BF16),
            pltpu.VMEM((2, heads, DV, DK), BF16),
            pltpu.VMEM((2, heads, DV, DK), BF16),
            pltpu.VMEM((heads, 2 * tok, DK), BF16),
            pltpu.VMEM((heads, tok, DV), F32),
            pltpu.VMEM((heads, tok, DV), BF16),
            pltpu.VMEM((heads, tok // 2, DV), BF16),
            pltpu.VMEM((tok // 2, wide), F32),
            dma((len(operands),)),
            dma((heads,)),
            dma((heads,)),
            dma((2 * heads,)),
            dma((heads,)),
            dma((2 * heads,)),
            dma((4 * heads,)),
            dma((2 * heads,)),
            dma((heads,)),
            dma((heads,)),
            dma((heads,)),
            dma(()),
            dma(()),
        ],
        compiler_params=pltpu.CompilerParams(vmem_limit_bytes=28 << 20, collective_id=0, has_side_effects=True),
        name="pair_project",
    )(*(pltpu.with_memory_space_constraint(x, pltpu.HBM) for x in operands))


def solution(mesh):
    in_specs = (
        P(("groups", "seq"), "head"),
        P(("groups", "seq"), None, "head"),
        P(("groups", "seq"), None, "head"),
        P("head", None, ("groups", "seq")),
        P("head", ("groups", "seq")),
        P(("groups", "seq")),
        P("head"),
        P("head", None),
    )
    out_specs = P(("groups", "seq", "head"), None)
    return jax.shard_map(shards, mesh=mesh, in_specs=in_specs, out_specs=out_specs, check_vma=False)
```
